512 devices in a mesh: blk: 64 (over z, x), day: 8 (over y, core).
Axes of the slice: x: 4, y: 4, z: 16, core: 2. Of those that a mesh axis runs over, the one named last changes fastest.
Arguments:
- input_field: float32 [2, 24, 512, 4096], P(None, 'day', 'blk'), may hold values from -6 to 6
- active_mask: int32 [512], P('blk'), may hold values from 0 to 1, as said below
- neighbours: int32 [512, 8], P('blk'), may hold values from -1 to 511, as said below
- time_taps: float32 [4], replicated, may hold values from 0.1 to 0.5
- space_taps: float32 [2, 5], replicated, may hold values from 0.1 to 0.5
- coregion_factor: float32 [2, 2], replicated, may hold values from -2.5 to 2.5
Outputs:
- covariance_product: float32 [2, 24, 512, 4096], P(None, 'day', 'blk')
The draws below stay inside these ranges and needn't reach their ends.
Inputs may be any that keep to these rules, and one draw needn't show every extreme that they name: `active_mask`: device i along blk holds in its 8 slots, in a drawn order, the map positions i * 8 to i * 8 + 7 of a map of 16 rows of 32 positions numbered row by row; every position of the first two map rows is active, others are active at random. Entries name the global slot (device index along blk times 8 plus local slot) of the active map block beside the block in that direction, -1 where there is none or it is inactive; all entries of an inactive slot are -1. East and west neighbours are held by the same device or one place away along blk; north and south ones by the device 4 places away; the four diagonal ones by the device 4 places away or one place nearer or farther than that, and all these cases occur.
All inputs are finite; a program needn't handle non-finite values.
Results may differ from the reference program's by a relative error of at most 0.0003.
Values sent between devices are 32-bit elements; how exact they have to be, the bound alone decides.
A program may use at most 64 MiB of HBM per device.

```python
import jax
import jax.numpy as jnp
from jax import lax

COMPS = 2
SIDE = 64
CELLS = 4096
SPACE_HALF = 4
TIME_HALF = 3
REACH = 4
BLOCKS_DEV = 8
DAYS = 24
SLOTS = 512
MAP_ROWS = 16
MAP_COLS = 32


def block_layout(key):
    devices_along = MAP_ROWS * REACH
    order_key, active_key = jax.random.split(jax.random.fold_in(key, 11))
    scores = jax.random.randint(order_key, (devices_along, BLOCKS_DEV), 0, 1048576) * BLOCKS_DEV + jnp.arange(BLOCKS_DEV, dtype=jnp.int32)[None, :]
    position_of_slot = jnp.argsort(scores, axis=1).astype(jnp.int32)
    slot_of_position = jnp.argsort(position_of_slot, axis=1).astype(jnp.int32)
    device_ids = jnp.arange(devices_along, dtype=jnp.int32)[:, None]
    global_position = (device_ids * BLOCKS_DEV + position_of_slot).reshape(-1)
    slot_at_position = (device_ids * BLOCKS_DEV + slot_of_position).reshape(-1)
    coins = jax.random.randint(active_key, (SLOTS,), 0, 10)
    map_row_of = jnp.arange(SLOTS, dtype=jnp.int32) // MAP_COLS
    active_at = ((coins < 8) | (map_row_of < 2)).astype(jnp.int32)
    active_slot = active_at[global_position]
    map_row = global_position // MAP_COLS
    map_col = global_position % MAP_COLS
    moves = [(0, 1), (0, -1), (-1, 0), (1, 0), (-1, 1), (-1, -1), (1, 1), (1, -1)]
    columns = []
    for row_move, col_move in moves:
        next_row = map_row + row_move
        next_col = map_col + col_move
        inside = (next_row >= 0) & (next_row < MAP_ROWS) & (next_col >= 0) & (next_col < MAP_COLS)
        next_position = jnp.clip(next_row, 0, MAP_ROWS - 1) * MAP_COLS + jnp.clip(next_col, 0, MAP_COLS - 1)
        usable = inside & (active_at[next_position] == 1) & (active_slot == 1)
        columns.append(jnp.where(usable, slot_at_position[next_position], -1))
    return (active_slot.astype(jnp.int32), jnp.stack(columns, axis=1).astype(jnp.int32))


def draw_active_mask(key, part):
    return block_layout(key)[0]


def draw_neighbours(key, part):
    return block_layout(key)[1]


def block_levels(own_key, extent, cuts, low, high):
    factor_of, own = 1.0, jax.random.fold_in(own_key, 6)
    for dim, parts in cuts:
        heights = jnp.exp(jax.random.uniform(jax.random.fold_in(own, dim), (parts,), jnp.float32, low / len(cuts), high / len(cuts)))
        factor_of = factor_of * jnp.repeat(heights, extent[dim] // parts).reshape([-1 if axis == dim else 1 for axis in range(len(extent))])
    return factor_of


def bell_draw(stream_key, extent, deviation, most, cuts=(), kind=jnp.bfloat16):
    gain = block_levels(stream_key, extent, cuts, -0.22, 0.18) if cuts else 1.0
    array = jax.random.normal(stream_key, extent, jnp.float32) * deviation * gain
    return jnp.minimum(jnp.maximum(array, -most), most).astype(kind)


def setup_inputs(seed: int = 0) -> dict:
    splits = jax.random.split(jax.random.key(seed), 7)
    return {
        "input_field": bell_draw(splits[0], (COMPS, DAYS, SLOTS, CELLS), 1.0, 6.0, ((1, 8), (2, 64)), jnp.float32),
        "active_mask": draw_active_mask(jax.random.fold_in(splits[6], 71), 0),
        "neighbours": draw_neighbours(jax.random.fold_in(splits[6], 71), 0),
        "time_taps": jnp.clip(jax.random.uniform(splits[3], (TIME_HALF + 1,), jnp.float32, 0.1, 0.5), 0.1, 0.5),
        "space_taps": jnp.clip(jax.random.uniform(splits[4], (2, SPACE_HALF + 1), jnp.float32, 0.1, 0.5), 0.1, 0.5),
        "coregion_factor": bell_draw(splits[5], (COMPS, COMPS), 0.8, 2.5, (), jnp.float32),
    }


def full_taps(tap_list, half_width):
    return [tap_list[abs(offset - half_width)] for offset in range(2 * half_width + 1)]


def coupling(coregion_factor):
    rows_list = []
    for first in range(2):
        rows_list.append(jnp.stack([coregion_factor[first, 0] * coregion_factor[second, 0] + coregion_factor[first, 1] * coregion_factor[second, 1] for second in range(2)]))
    return jnp.stack(rows_list)


def mix_outputs(weights, filtered):
    return jnp.stack([weights[0, 0] * filtered[0] + weights[0, 1] * filtered[1], weights[1, 0] * filtered[0] + weights[1, 1] * filtered[1]])


def cut_strips(blocks, half_width):
    leading = blocks.shape[:-2]
    east_strip = blocks[..., :, blocks.shape[-1] - half_width:]
    west_strip = blocks[..., :, :half_width]
    north_strip = blocks[..., :half_width, :]
    south_strip = blocks[..., blocks.shape[-2] - half_width:, :]
    return [strip_piece.reshape(leading + (-1,)) for strip_piece in (east_strip, west_strip, north_strip, south_strip)]


def frame(blocks, fetch_strip, half_width, block_side):
    leading = blocks.shape[:-2]
    east_face = fetch_strip(0, 1).reshape(leading + (block_side, half_width))
    west_face = fetch_strip(1, 0).reshape(leading + (block_side, half_width))
    north_face = fetch_strip(2, 3).reshape(leading + (half_width, block_side))
    south_face = fetch_strip(3, 2).reshape(leading + (half_width, block_side))
    north_east = fetch_strip(4, 3).reshape(leading + (half_width, block_side))[..., :half_width]
    north_west = fetch_strip(5, 3).reshape(leading + (half_width, block_side))[..., block_side - half_width:]
    south_east = fetch_strip(6, 2).reshape(leading + (half_width, block_side))[..., :half_width]
    south_west = fetch_strip(7, 2).reshape(leading + (half_width, block_side))[..., block_side - half_width:]
    upper_rows = jnp.concatenate([north_west, north_face, north_east], axis=-1)
    middle = jnp.concatenate([west_face, blocks, east_face], axis=-1)
    bottom = jnp.concatenate([south_west, south_face, south_east], axis=-1)
    return jnp.concatenate([upper_rows, middle, bottom], axis=-2)


def smooth(padded, taps_across, taps_down, block_side):
    across = None
    for offset in range(len(taps_across)):
        addend = taps_across[offset] * padded[..., :, offset:offset + block_side]
        across = addend if across is None else across + addend
    downward = None
    for offset in range(len(taps_down)):
        addend = taps_down[offset] * across[..., offset:offset + block_side, :]
        downward = addend if downward is None else downward + addend
    return downward


def reference(input_field, active_mask, neighbours, time_taps, space_taps, coregion_factor):
    live_mask = active_mask.astype(jnp.float32)
    weights = coupling(coregion_factor)
    taps_across = full_taps(space_taps[0], SPACE_HALF)
    taps_down = full_taps(space_taps[1], SPACE_HALF)

    def one_day(day_index):
        filtered = None
        for offset in range(-TIME_HALF, TIME_HALF + 1):
            shifted = day_index + offset
            inside = ((shifted >= 0) & (shifted < DAYS)).astype(jnp.float32)
            picked = lax.dynamic_index_in_dim(input_field, jnp.clip(shifted, 0, DAYS - 1).astype(jnp.int32), 1, keepdims=False)
            addend = (time_taps[abs(offset)] * inside) * (picked * live_mask[None, :, None])
            filtered = addend if filtered is None else filtered + addend
        mixed_field = mix_outputs(weights, filtered)
        blocks = mixed_field.reshape((COMPS, SLOTS, SIDE, SIDE))
        strip_list = cut_strips(blocks, SPACE_HALF)

        def fetch_strip(direction, strip):
            target = neighbours[:, direction]
            present = (target >= 0).astype(jnp.float32)[None, :, None]
            return jnp.take(strip_list[strip], jnp.clip(target, 0, SLOTS - 1), axis=1) * present

        padded = frame(blocks, fetch_strip, SPACE_HALF, SIDE)
        result = smooth(padded, taps_across, taps_down, SIDE)
        return result.reshape((COMPS, SLOTS, CELLS)) * live_mask[None, :, None]

    stacked = lax.map(one_day, jnp.arange(DAYS, dtype=jnp.int32))
    return jnp.moveaxis(stacked, 0, 1)
```

```python
import functools

import jax
import jax.numpy as jnp
from jax import lax
from jax.experimental import pallas as pl
from jax.experimental.pallas import tpu as pltpu
from jax.sharding import PartitionSpec as P

MESH = pl.DeviceIdType.MESH
REACH = 4
SLOTS = 8
DAYS = 3
SERIES = 2 * DAYS
TILES = 32
ROWS = TILES * SLOTS
STEP = 4
CHUNKS = (TILES - 4) // STEP
NONE = -(1 << 20)

EAST, WEST, NORTH, SOUTH, NE, NW, SE, SW = range(8)
PLACES = ((1, 0), (-1, 0), (1, -1), (-1, -1), (1, 1), (-1, 1))
OPPOSITE = (1, 0, 5, 4, 3, 2)


def kernel(
    x_hbm, nbr, act, time_taps, space_taps, factor, out_hbm,
    own, left, right, pack, pack_left, pack_right, pack_mixed, packs,
    mixed, strip_n, strip_s, halo, across, swapped, done,
    in_mask, north_mask, north_side, south_mask, south_side, edge_mask, pack_mask, live_mask,
    load_sem, y_send, y_recv, z_send, z_recv, p_send, p_recv, out_sem,
):
    f32 = jnp.float32
    blk, day = lax.axis_index("blk"), lax.axis_index("day")
    blks, days = lax.axis_size("blk"), lax.axis_size("day")
    col, row, rows = blk % REACH, blk // REACH, blks // REACH

    has_left, has_right = day > 0, day < days - 1
    has_north, has_south = row > 0, row < rows - 1

    def place_exists(dx, dz):
        ok = (col + dx >= 0) & (col + dx < REACH)
        if dz:
            ok = ok & (row + dz >= 0) & (row + dz < rows)
        return ok

    partners = [(has_left, 0, -1), (has_right, 0, 1), (has_north, -REACH, 0), (has_south, REACH, 0)]
    for dx, dz in PLACES:
        partners.append((place_exists(dx, dz), dx + REACH * dz, 0))

    load = pltpu.make_async_copy(x_hbm, own, load_sem)
    load.start()
    barrier = pltpu.get_barrier_semaphore()
    expected = 0
    for there, db, dd in partners:
        @pl.when(there)
        def _(db=db, dd=dd):
            pl.semaphore_signal(
                barrier, inc=1, device_id={"blk": blk + db, "day": day + dd}, device_id_type=MESH
            )
        expected = expected + there.astype(jnp.int32)

    lane = lax.broadcasted_iota(jnp.int32, (SLOTS, 128), 1)
    cell = lane & 63
    low, high = cell < 4, cell >= 60
    slot = lax.broadcasted_iota(jnp.int32, (SLOTS, 128), 0)

    def named(direction):
        column = jnp.broadcast_to(nbr[:, direction : direction + 1], (SLOTS, 128))
        return jnp.where(column < 0, NONE, column)

    def on(target, db):
        first = (blk + db) * SLOTS
        return (target >= first) & (target < first + SLOTS)

    def sides(east, west):
        return jnp.where(low, named(east), jnp.where(high, named(west), NONE))

    def picks(ref, target, db):
        first = (blk + db) * SLOTS
        for s in range(SLOTS):
            ref[s] = jnp.where(target == first + s, 1.0, 0.0).astype(f32)

    picks(in_mask, sides(EAST, WEST), 0)
    picks(north_mask, named(NORTH), -REACH)
    picks(north_side, sides(NE, NW), -REACH)
    picks(south_mask, named(SOUTH), REACH)
    picks(south_side, sides(SE, SW), REACH)
    for index, (east, west, dz) in enumerate(((EAST, WEST, 0), (NE, NW, -1), (SE, SW, 1))):
        there = (low & on(named(east), REACH * dz + 1)) | (high & on(named(west), REACH * dz - 1))
        edge_mask[index] = jnp.where(there, 1.0, 0.0).astype(f32)
    at_east = on(named(EAST), 1) | on(named(NE), 1 - REACH) | on(named(SE), 1 + REACH)
    at_west = on(named(WEST), -1) | on(named(NW), -1 - REACH) | on(named(SW), -1 + REACH)
    pack_mask[...] = jnp.where((high & at_east) | (low & at_west), 1.0, 0.0).astype(f32)
    live = jnp.zeros((SLOTS, 128), f32)
    for s in range(SLOTS):
        live = jnp.where(slot == s, act[s].astype(f32), live)
    live_mask[...] = live

    load.wait()

    for t in range(DAYS):
        total = jnp.zeros((SLOTS, 128), f32)
        for c in range(2):
            for q in range(4):
                part = jnp.zeros((SLOTS, 128), f32)
                for s in range(SLOTS):
                    part = part + (
                        own[c * DAYS + t, pl.ds(q * SLOTS + s, SLOTS, stride=4 * SLOTS), :]
                        * pack_mask[s : s + 1, :]
                    )
                shift = 8 * (4 * c + q)
                total = total + (pltpu.roll(part, shift, 1) if shift else part)
        pack[t * SLOTS : (t + 1) * SLOTS, :] = total

    @pl.when(jnp.logical_not(has_left))
    def _():
        pack_left[...] = jnp.zeros_like(pack_left)

        def clear(i, carry):
            left[i] = jnp.zeros((ROWS, 128), f32)
            return carry

        lax.fori_loop(0, SERIES, clear, 0)

    @pl.when(jnp.logical_not(has_right))
    def _():
        pack_right[...] = jnp.zeros_like(pack_right)

        def clear(i, carry):
            right[i] = jnp.zeros((ROWS, 128), f32)
            return carry

        lax.fori_loop(0, SERIES, clear, 0)

    @pl.when(jnp.logical_not(has_north))
    def _():
        strip_n[...] = jnp.zeros_like(strip_n)

    @pl.when(jnp.logical_not(has_south))
    def _():
        strip_s[...] = jnp.zeros_like(strip_s)

    for index, (dx, dz) in enumerate(PLACES):
        @pl.when(jnp.logical_not(place_exists(dx, dz)))
        def _(index=index):
            packs[index] = jnp.zeros((DAYS * SLOTS, 128), f32)

    pl.semaphore_wait(barrier, expected)

    def y_copy(side, item):
        target = left if side == 0 else right
        if isinstance(item, int) and item == 0:
            source, target = pack, (pack_left if side == 0 else pack_right)
        else:
            if isinstance(item, int):
                span = pl.ds(0 if item == 1 else ROWS - 16, 16)
            else:
                span = pl.ds(pl.multiple_of(16 + (item - 3) * (STEP * SLOTS), 8), STEP * SLOTS)
            source, target = x_hbm.at[:, span, :], target.at[:, span, :]
        return pltpu.make_async_remote_copy(
            src_ref=source, dst_ref=target,
            send_sem=y_send.at[side, item], recv_sem=y_recv.at[side, item],
            device_id={"blk": blk, "day": day + (1 if side == 0 else -1)}, device_id_type=MESH,
        )

    for side, there in ((0, has_right), (1, has_left)):
        @pl.when(there)
        def _(side=side):
            for item in range(3):
                y_copy(side, item).start()

            def send(j, carry):
                y_copy(side, j).start()
                return carry

            lax.fori_loop(3, 3 + CHUNKS, send, 0)

    def y_wait(item):
        for side, there in ((0, has_left), (1, has_right)):
            @pl.when(there)
            def _(side=side):
                y_copy(side, item).wait_recv()

    w = [time_taps[k] for k in range(DAYS + 1)]
    a = [space_taps[0, k] for k in range(5)]
    d = [space_taps[1, k] for k in range(5)]
    k00 = factor[0, 0] * factor[0, 0] + factor[0, 1] * factor[0, 1]
    k01 = factor[0, 0] * factor[1, 0] + factor[0, 1] * factor[1, 1]
    k11 = factor[1, 0] * factor[1, 0] + factor[1, 1] * factor[1, 1]

    def filtered(v):
        return [
            w[0] * v[t + 3] + w[1] * (v[t + 2] + v[t + 4])
            + w[2] * (v[t + 1] + v[t + 5]) + w[3] * (v[t] + v[t + 6])
            for t in range(DAYS)
        ]

    def mix_tile(at):
        span = pl.ds(at, SLOTS)
        f = []
        for c in range(2):
            v = [ref[c * DAYS + t, span, :] for ref in (left, own, right) for t in range(DAYS)]
            f.append(filtered(v))
        m = live_mask[...]
        for t in range(DAYS):
            mixed[t, span, :] = (k00 * f[0][t] + k01 * f[1][t]) * m
            mixed[DAYS + t, span, :] = (k01 * f[0][t] + k11 * f[1][t]) * m

    for item in range(3):
        y_wait(item)
    v = [
        ref[t * SLOTS : (t + 1) * SLOTS, :]
        for ref in (pack_left, pack, pack_right) for t in range(DAYS)
    ]
    second = (((lane + 68) >> 3) & 7) >= 4
    for t, f in enumerate(filtered(v)):
        first_part = k00 * f + k01 * pltpu.roll(f, 96, 1)
        second_part = k11 * f + k01 * pltpu.roll(f, 32, 1)
        pack_mixed[t * SLOTS : (t + 1) * SLOTS, :] = jnp.where(second, second_part, first_part)
    for tile in (0, 1, TILES - 2, TILES - 1):
        mix_tile(tile * SLOTS)

    def p_copy(index):
        dx, dz = PLACES[index]
        return pltpu.make_async_remote_copy(
            src_ref=pack_mixed, dst_ref=packs.at[OPPOSITE[index]],
            send_sem=p_send.at[index], recv_sem=p_recv.at[OPPOSITE[index]],
            device_id={"blk": blk + dx + REACH * dz, "day": day}, device_id_type=MESH,
        )

    def p_arrival(index):
        return pltpu.make_async_remote_copy(
            src_ref=pack_mixed, dst_ref=packs.at[index],
            send_sem=p_send.at[index], recv_sem=p_recv.at[index],
            device_id={"blk": blk, "day": day}, device_id_type=MESH,
        )

    def z_copy(side):
        span = pl.ds(ROWS - 16, 16) if side == 0 else pl.ds(0, 16)
        return pltpu.make_async_remote_copy(
            src_ref=mixed.at[:, span, :], dst_ref=strip_n if side == 0 else strip_s,
            send_sem=z_send.at[side], recv_sem=z_recv.at[side],
            device_id={"blk": blk + (REACH if side == 0 else -REACH), "day": day},
            device_id_type=MESH,
        )

    for index, (dx, dz) in enumerate(PLACES):
        @pl.when(place_exists(dx, dz))
        def _(index=index):
            p_copy(index).start()

    for side, there in ((0, has_south), (1, has_north)):
        @pl.when(there)
        def _(side=side):
            z_copy(side).start()

    for index, (dx, dz) in enumerate(PLACES):
        @pl.when(place_exists(dx, dz))
        def _(index=index):
            p_arrival(index).wait_recv()

    for side, there in ((0, has_north), (1, has_south)):
        @pl.when(there)
        def _(side=side):
            z_copy(side).wait_recv()

    west_lanes = (lane & 7) < 4
    for t in range(DAYS):
        span = slice(t * SLOTS, (t + 1) * SLOTS)
        for index in range(3):
            both = jnp.where(west_lanes, packs[2 * index, span, :], packs[2 * index + 1, span, :])
            for c in range(2):
                for q in range(4):
                    shift = 8 * (4 * c + q)
                    value = pltpu.roll(both, 128 - shift, 1) if shift else both
                    halo[index, c * DAYS + t, q] = value

    def pick(ref, series, at, masks):
        total = None
        for s in range(SLOTS):
            term = ref[series, pl.ds(at + s, 1), :] * masks[s]
            total = term if total is None else total + term
        return total

    def filter_across(centre, side, series, at):
        turned = pltpu.roll(side, 64, 1)
        total = a[0] * centre
        for k in range(1, 5):
            ahead = pltpu.roll(jnp.where(cell < k, turned, centre), 128 - k, 1)
            behind = pltpu.roll(jnp.where(cell >= 64 - k, turned, centre), k, 1)
            total = total + a[k] * (ahead + behind)
        span = pl.ds(at, SLOTS)
        across[series, span, :] = total
        swapped[series, span, :] = pltpu.roll(total, 64, 1)

    def own_across(series, tile, g, q):
        at = tile * SLOTS
        side = pick(mixed, series, at, in_mask)
        side = side + halo[0, series, q, pl.ds(g, 1), :] * edge_mask[0]
        filter_across(mixed[series, pl.ds(at, SLOTS), :], side, series, at + 2 * SLOTS)

    def edges_across(series, carry):
        for tile in (0, 1, TILES - 2, TILES - 1):
            own_across(series, tile, tile // 4, tile % 4)
        for n in range(2):
            tile = TILES - 2 + n
            centre = pick(strip_n, series, n * SLOTS, north_mask)
            side = pick(strip_n, series, n * SLOTS, north_side)
            side = side + halo[1, series, tile % 4, pl.ds(tile // 4, 1), :] * edge_mask[1]
            filter_across(centre, side, series, n * SLOTS)
            centre = pick(strip_s, series, n * SLOTS, south_mask)
            side = pick(strip_s, series, n * SLOTS, south_side)
            side = side + halo[2, series, n, pl.ds(0, 1), :] * edge_mask[2]
            filter_across(centre, side, series, (TILES + 2 + n) * SLOTS)
        return carry

    lax.fori_loop(0, SERIES, edges_across, 0)

    first_half = lane < 64

    def filter_down(series, tile):
        base = tile * SLOTS
        m = live_mask[...]
        s = [across[series, pl.ds(base + SLOTS * n, SLOTS), :] for n in range(STEP + 4)]
        b = [swapped[series, pl.ds(base + SLOTS * n, SLOTS), :] for n in range(STEP + 4)]
        o = [jnp.where(first_half, b[n], b[n + 1]) for n in range(STEP + 3)]
        for n in range(STEP):
            total = (
                d[0] * s[n + 2] + d[1] * (o[n + 2] + o[n + 1]) + d[2] * (s[n + 3] + s[n + 1])
                + d[3] * (o[n + 3] + o[n]) + d[4] * (s[n + 4] + s[n])
            )
            done[series, pl.ds(base + SLOTS * n, SLOTS), :] = total * m

    def out_copy(chunk):
        span = pl.ds(pl.multiple_of(chunk * (STEP * SLOTS), 8), STEP * SLOTS)
        return pltpu.make_async_copy(
            done.at[:, span, :], out_hbm.at[:, span, :], out_sem.at[chunk]
        )

    def bulk(j, carry):
        y_wait(j + 3)
        first = pl.multiple_of(16 + j * (STEP * SLOTS), 8)
        for n in range(STEP):
            mix_tile(first + n * SLOTS)

        def series_step(series, inner):
            for n in range(STEP):
                own_across(series, 2 + j * STEP + n, j + (2 + n) // 4, (2 + n) % 4)
            filter_down(series, j * STEP)
            return inner

        lax.fori_loop(0, SERIES, series_step, 0)
        out_copy(j).start()
        return carry

    lax.fori_loop(0, CHUNKS, bulk, 0)

    def last_step(series, carry):
        filter_down(series, TILES - STEP)
        return carry

    lax.fori_loop(0, SERIES, last_step, 0)
    out_copy(CHUNKS).start()

    for side, there in ((0, has_right), (1, has_left)):
        @pl.when(there)
        def _(side=side):
            for item in range(3):
                y_copy(side, item).wait_send()

            def sent(j, carry):
                y_copy(side, j).wait_send()
                return carry

            lax.fori_loop(3, 3 + CHUNKS, sent, 0)

    for index, (dx, dz) in enumerate(PLACES):
        @pl.when(place_exists(dx, dz))
        def _(index=index):
            p_copy(index).wait_send()

    for side, there in ((0, has_south), (1, has_north)):
        @pl.when(there)
        def _(side=side):
            z_copy(side).wait_send()

    def written(chunk, carry):
        out_copy(chunk).wait()
        return carry

    lax.fori_loop(0, CHUNKS + 1, written, 0)


def shards(input_field, active_mask, neighbours, time_taps, space_taps, coregion_factor):
    shape = input_field.shape
    tiles = input_field.reshape(2, DAYS, SLOTS, TILES, 128).transpose(0, 1, 3, 2, 4)
    tiles = tiles.reshape(SERIES, ROWS, 128)
    f32 = jnp.float32
    vmem = pltpu.VMEM
    smem = pl.BlockSpec(memory_space=pltpu.SMEM)
    dma = pltpu.SemaphoreType.DMA
    out = pl.pallas_call(
        kernel,
        out_shape=jax.ShapeDtypeStruct((SERIES, ROWS, 128), f32),
        in_specs=[
            pl.BlockSpec(memory_space=pl.ANY),
            pl.BlockSpec(memory_space=pltpu.VMEM),
            smem, smem, smem, smem,
        ],
        out_specs=pl.BlockSpec(memory_space=pl.ANY),
        scratch_shapes=[
            vmem((SERIES, ROWS, 128), f32),
            vmem((SERIES, ROWS, 128), f32),
            vmem((SERIES, ROWS, 128), f32),
            vmem((DAYS * SLOTS, 128), f32),
            vmem((DAYS * SLOTS, 128), f32),
            vmem((DAYS * SLOTS, 128), f32),
            vmem((DAYS * SLOTS, 128), f32),
            vmem((6, DAYS * SLOTS, 128), f32),
            vmem((SERIES, ROWS, 128), f32),
            vmem((SERIES, 16, 128), f32),
            vmem((SERIES, 16, 128), f32),
            vmem((3, SERIES, 4, SLOTS, 128), f32),
            vmem((SERIES, ROWS + 32, 128), f32),
            vmem((SERIES, ROWS + 32, 128), f32),
            vmem((SERIES, ROWS, 128), f32),
            vmem((SLOTS, SLOTS, 128), f32),
            vmem((SLOTS, SLOTS, 128), f32),
            vmem((SLOTS, SLOTS, 128), f32),
            vmem((SLOTS, SLOTS, 128), f32),
            vmem((SLOTS, SLOTS, 128), f32),
            vmem((3, SLOTS, 128), f32),
            vmem((SLOTS, 128), f32),
            vmem((SLOTS, 128), f32),
            dma,
            dma((2, 3 + CHUNKS)),
            dma((2, 3 + CHUNKS)),
            dma((2,)),
            dma((2,)),
            dma((6,)),
            dma((6,)),
            dma((CHUNKS + 1,)),
        ],
        compiler_params=pltpu.CompilerParams(collective_id=0, has_side_effects=True),
    )(tiles, neighbours, active_mask, time_taps, space_taps, coregion_factor)
    out = out.reshape(2, DAYS, TILES, SLOTS, 128).transpose(0, 1, 3, 2, 4)
    return out.reshape(shape)


def solution(mesh):
    in_specs = (P(None, "day", "blk", None), P("blk"), P("blk", None), P(), P(), P())
    out_specs = P(None, "day", "blk", None)
    return jax.shard_map(shards, mesh=mesh, in_specs=in_specs, out_specs=out_specs, check_vma=False)
```

```python
import functools

import jax
import jax.numpy as jnp
from jax import lax
from jax.experimental import pallas as pl
from jax.experimental.pallas import tpu as pltpu
from jax.sharding import PartitionSpec as P

MESH = pl.DeviceIdType.MESH
REACH = 4
SLOTS = 8
DAYS = 3
SERIES = 2 * DAYS
TILES = 32
ROWS = TILES * SLOTS
STEP = 4
CHUNKS = (TILES - 4) // STEP
AHEAD = 1
NONE = -(1 << 20)

EAST, WEST, NORTH, SOUTH, NE, NW, SE, SW = range(8)
PLACES = ((1, 0), (-1, 0), (1, -1), (-1, -1), (1, 1), (-1, 1))
OPPOSITE = (1, 0, 5, 4, 3, 2)


def kernel(
    x_hbm, nbr, act, time_taps, space_taps, factor, out_hbm,
    own, left, right, pack, pack_left, pack_right, pack_mixed, packs,
    mixed, strip_n, strip_s, halo, lhs, weights, across, swapped, done,
    take_index, take_mask, edge_mask, live_mask,
    load_sem, y_send, y_recv, z_send, z_recv, p_send, p_recv, out_sem,
):
    f32, bf16 = jnp.float32, jnp.bfloat16
    blk, day = lax.axis_index("blk"), lax.axis_index("day")
    blks, days = lax.axis_size("blk"), lax.axis_size("day")
    col, row, rows = blk % REACH, blk // REACH, blks // REACH

    has_left, has_right = day > 0, day < days - 1
    has_north, has_south = row > 0, row < rows - 1

    def place_exists(dx, dz):
        ok = (col + dx >= 0) & (col + dx < REACH)
        if dz:
            ok = ok & (row + dz >= 0) & (row + dz < rows)
        return ok

    partners = [(has_left, 0, -1), (has_right, 0, 1), (has_north, -REACH, 0), (has_south, REACH, 0)]
    for dx, dz in PLACES:
        partners.append((place_exists(dx, dz), dx + REACH * dz, 0))

    load = pltpu.make_async_copy(x_hbm, own, load_sem)
    load.start()
    barrier = pltpu.get_barrier_semaphore()
    expected = 0
    for there, db, dd in partners:
        @pl.when(there)
        def _(db=db, dd=dd):
            pl.semaphore_signal(
                barrier, inc=1, device_id={"blk": blk + db, "day": day + dd}, device_id_type=MESH
            )
        expected = expected + there.astype(jnp.int32)

    lane = lax.broadcasted_iota(jnp.int32, (SLOTS, 128), 1)
    cell = lane & 63
    low, high = cell < 4, cell >= 60
    slot = lax.broadcasted_iota(jnp.int32, (SLOTS, 128), 0)

    def named(direction):
        column = jnp.broadcast_to(nbr[:, direction : direction + 1], (SLOTS, 128))
        return jnp.where(column < 0, NONE, column)

    def on(target, db):
        first = (blk + db) * SLOTS
        return (target >= first) & (target < first + SLOTS)

    def sides(east, west):
        return jnp.where(low, named(east), jnp.where(high, named(west), NONE))

    for index, (target, db) in enumerate((
        (sides(EAST, WEST), 0),
        (named(NORTH), -REACH), (sides(NE, NW), -REACH),
        (named(SOUTH), REACH), (sides(SE, SW), REACH),
    )):
        take_index[index] = target & (SLOTS - 1)
        take_mask[index] = jnp.where(on(target, db), 1.0, 0.0).astype(f32)
    for index, (east, west, dz) in enumerate(((EAST, WEST, 0), (NE, NW, -1), (SE, SW, 1))):
        there = (low & on(named(east), REACH * dz + 1)) | (high & on(named(west), REACH * dz - 1))
        edge_mask[index] = jnp.where(there, 1.0, 0.0).astype(f32)
    at_east = on(named(EAST), 1) | on(named(NE), 1 - REACH) | on(named(SE), 1 + REACH)
    at_west = on(named(WEST), -1) | on(named(NW), -1 - REACH) | on(named(SW), -1 + REACH)
    ends = jnp.where((high & at_east) | (low & at_west), 1.0, 0.0).astype(f32)
    end_slot = jnp.broadcast_to(
        jnp.sum(ends * slot.astype(f32), axis=0, keepdims=True), (SLOTS, 128)
    ).astype(jnp.int32)
    end_mask = jnp.broadcast_to(jnp.sum(ends, axis=0, keepdims=True), (SLOTS, 128))
    live = jnp.zeros((SLOTS, 128), f32)
    for s in range(SLOTS):
        live = jnp.where(slot == s, act[s].astype(f32), live)
    live_mask[...] = live

    @pl.when(jnp.logical_not(has_left))
    def _():
        pack_left[...] = jnp.zeros_like(pack_left)

        def clear(i, carry):
            left[i] = jnp.zeros((ROWS, 128), f32)
            return carry

        lax.fori_loop(0, SERIES, clear, 0)

    @pl.when(jnp.logical_not(has_right))
    def _():
        pack_right[...] = jnp.zeros_like(pack_right)

        def clear(i, carry):
            right[i] = jnp.zeros((ROWS, 128), f32)
            return carry

        lax.fori_loop(0, SERIES, clear, 0)

    @pl.when(jnp.logical_not(has_north))
    def _():
        strip_n[...] = jnp.zeros_like(strip_n)

    @pl.when(jnp.logical_not(has_south))
    def _():
        strip_s[...] = jnp.zeros_like(strip_s)

    for index, (dx, dz) in enumerate(PLACES):
        @pl.when(jnp.logical_not(place_exists(dx, dz)))
        def _(index=index):
            packs[index] = jnp.zeros((DAYS * SLOTS, 128), f32)

    pl.semaphore_wait(barrier, expected)

    def bulk_row(j):
        at = 16 + j * (STEP * SLOTS)
        return at if isinstance(j, int) else pl.multiple_of(at, 8)

    def y_copy(side, item):
        target = left if side == 0 else right
        if isinstance(item, int) and item == 0:
            source, target = pack, (pack_left if side == 0 else pack_right)
        else:
            if isinstance(item, int) and item < 3:
                span = pl.ds(0 if item == 1 else ROWS - 16, 16)
            else:
                span = pl.ds(bulk_row(item - 3), STEP * SLOTS)
            source, target = x_hbm.at[:, span, :], target.at[:, span, :]
        return pltpu.make_async_remote_copy(
            src_ref=source, dst_ref=target,
            send_sem=y_send.at[side, item], recv_sem=y_recv.at[side, item],
            device_id={"blk": blk, "day": day + (1 if side == 0 else -1)}, device_id_type=MESH,
        )

    for side, there in ((0, has_right), (1, has_left)):
        @pl.when(there)
        def _(side=side):
            for item in range(1, 3 + AHEAD):
                y_copy(side, item).start()

    load.wait()

    for t in range(DAYS):
        total = jnp.zeros((SLOTS, 128), f32)
        for c in range(2):
            for q in range(4):
                part = None
                for g in range(SLOTS):
                    value = own[c * DAYS + t, pl.ds((4 * g + q) * SLOTS, SLOTS), :]
                    value = jnp.take_along_axis(value, end_slot, axis=0)
                    part = value if part is None else jnp.where(slot == g, value, part)
                part = part * end_mask
                shift = 8 * (4 * c + q)
                total = total + (pltpu.roll(part, shift, 1) if shift else part)
        pack[t * SLOTS : (t + 1) * SLOTS, :] = total

    for side, there in ((0, has_right), (1, has_left)):
        @pl.when(there)
        def _(side=side):
            y_copy(side, 0).start()

            def send(j, carry):
                y_copy(side, j).start()
                return carry

            lax.fori_loop(3 + AHEAD, 3 + CHUNKS, send, 0)

    def y_wait(item):
        for side, there in ((0, has_left), (1, has_right)):
            @pl.when(there)
            def _(side=side):
                y_copy(side, item).wait_recv()

    w = [time_taps[k] for k in range(DAYS + 1)]
    a = [space_taps[0, k] for k in range(5)]
    d = [space_taps[1, k] for k in range(5)]
    k00 = factor[0, 0] * factor[0, 0] + factor[0, 1] * factor[0, 1]
    k01 = factor[0, 0] * factor[1, 0] + factor[0, 1] * factor[1, 1]
    k11 = factor[1, 0] * factor[1, 0] + factor[1, 1] * factor[1, 1]

    k = lax.broadcasted_iota(jnp.int32, (256, 256), 0)
    n = lax.broadcasted_iota(jnp.int32, (256, 256), 1)
    place = k & 63
    beyond = jnp.where(place < 4, place + 64, jnp.where(place >= 60, place - 64, 1024))
    place = jnp.where(k >= 128, beyond, place)
    distance = jnp.abs(place - (n & 63))
    same_row = ((k >> 6) & 1) == (((n >> 6) ^ (n >> 7)) & 1)
    weight = jnp.zeros((256, 256), f32)
    for tap in range(5):
        weight = jnp.where(same_row & (distance == tap), a[tap], weight)
    weight_high = weight.astype(bf16)
    weights[0:256, :] = weight_high
    weights[256:512, :] = weight_high
    weights[512:768, :] = (weight - weight_high.astype(f32)).astype(bf16)

    def filtered(v):
        return [
            w[0] * v[t + 3] + w[1] * (v[t + 2] + v[t + 4])
            + w[2] * (v[t + 1] + v[t + 5]) + w[3] * (v[t] + v[t + 6])
            for t in range(DAYS)
        ]

    def mix_tile(at):
        span = pl.ds(at, SLOTS)
        f = []
        for c in range(2):
            v = [ref[c * DAYS + t, span, :] for ref in (left, own, right) for t in range(DAYS)]
            f.append(filtered(v))
        m = live_mask[...]
        for t in range(DAYS):
            mixed[t, span, :] = (k00 * f[0][t] + k01 * f[1][t]) * m
            mixed[DAYS + t, span, :] = (k01 * f[0][t] + k11 * f[1][t]) * m

    for item in range(3):
        y_wait(item)
    v = [
        ref[t * SLOTS : (t + 1) * SLOTS, :]
        for ref in (pack_left, pack, pack_right) for t in range(DAYS)
    ]
    second = (((lane + 68) >> 3) & 7) >= 4
    for t, f in enumerate(filtered(v)):
        first_part = k00 * f + k01 * pltpu.roll(f, 96, 1)
        second_part = k11 * f + k01 * pltpu.roll(f, 32, 1)
        pack_mixed[t * SLOTS : (t + 1) * SLOTS, :] = jnp.where(second, second_part, first_part)
    for tile in (0, 1, TILES - 2, TILES - 1):
        mix_tile(tile * SLOTS)

    def p_copy(index):
        dx, dz = PLACES[index]
        return pltpu.make_async_remote_copy(
            src_ref=pack_mixed, dst_ref=packs.at[OPPOSITE[index]],
            send_sem=p_send.at[index], recv_sem=p_recv.at[OPPOSITE[index]],
            device_id={"blk": blk + dx + REACH * dz, "day": day}, device_id_type=MESH,
        )

    def p_arrival(index):
        return pltpu.make_async_remote_copy(
            src_ref=pack_mixed, dst_ref=packs.at[index],
            send_sem=p_send.at[index], recv_sem=p_recv.at[index],
            device_id={"blk": blk, "day": day}, device_id_type=MESH,
        )

    def z_copy(side):
        span = pl.ds(ROWS - 16, 16) if side == 0 else pl.ds(0, 16)
        return pltpu.make_async_remote_copy(
            src_ref=mixed.at[:, span, :], dst_ref=strip_n if side == 0 else strip_s,
            send_sem=z_send.at[side], recv_sem=z_recv.at[side],
            device_id={"blk": blk + (REACH if side == 0 else -REACH), "day": day},
            device_id_type=MESH,
        )

    for index, (dx, dz) in enumerate(PLACES):
        @pl.when(place_exists(dx, dz))
        def _(index=index):
            p_copy(index).start()

    for side, there in ((0, has_south), (1, has_north)):
        @pl.when(there)
        def _(side=side):
            z_copy(side).start()

    for index, (dx, dz) in enumerate(PLACES):
        @pl.when(place_exists(dx, dz))
        def _(index=index):
            p_arrival(index).wait_recv()

    for side, there in ((0, has_north), (1, has_south)):
        @pl.when(there)
        def _(side=side):
            z_copy(side).wait_recv()

    west_lanes = (lane & 7) < 4
    for t in range(DAYS):
        span = slice(t * SLOTS, (t + 1) * SLOTS)
        for index in range(3):
            both = jnp.where(west_lanes, packs[2 * index, span, :], packs[2 * index + 1, span, :])
            for c in range(2):
                for q in range(4):
                    shift = 8 * (4 * c + q)
                    value = pltpu.roll(both, 128 - shift, 1) if shift else both
                    halo[index, c * DAYS + t, q] = value

    def take(value, index):
        return jnp.take_along_axis(value, take_index[index], axis=0) * take_mask[index]

    def own_side(series, at, g, q):
        side = take(mixed[series, pl.ds(at, SLOTS), :], 0)
        return side + halo[0, series, q, pl.ds(g, 1), :] * edge_mask[0]

    def stage(series, centres, side_tiles):
        span = pl.ds(pl.multiple_of(series * (STEP * SLOTS), 8), STEP * SLOTS)
        for column, value in ((0, centres), (128, jnp.concatenate(side_tiles, axis=0))):
            top = value.astype(bf16)
            rest = (value - top.astype(f32)).astype(bf16)
            lhs[span, column : column + 128] = top
            lhs[span, 256 + column : 384 + column] = rest
            lhs[span, 512 + column : 640 + column] = top

    def filter_across(at):
        result = jnp.dot(lhs[...], weights[...], preferred_element_type=f32)
        for series in range(SERIES):
            part = result[series * STEP * SLOTS : (series + 1) * STEP * SLOTS]
            across[series, pl.ds(at, STEP * SLOTS), :] = part[:, :128]
            swapped[series, pl.ds(at, STEP * SLOTS), :] = part[:, 128:]

    def north_stage(series, carry):
        centres, side_tiles = [], []
        for tile in range(2):
            value = strip_n[series, tile * SLOTS : (tile + 1) * SLOTS, :]
            centres.append(take(value, 1))
            edge = halo[1, series, 2 + tile, SLOTS - 1 : SLOTS, :] * edge_mask[1]
            side_tiles.append(take(value, 2) + edge)
        for tile in range(2):
            centres.append(mixed[series, tile * SLOTS : (tile + 1) * SLOTS, :])
            side_tiles.append(own_side(series, tile * SLOTS, 0, tile))
        stage(series, jnp.concatenate(centres, axis=0), side_tiles)
        return carry

    def south_stage(series, carry):
        centres, side_tiles = [], []
        for tile in range(TILES - 2, TILES):
            centres.append(mixed[series, tile * SLOTS : (tile + 1) * SLOTS, :])
            side_tiles.append(own_side(series, tile * SLOTS, SLOTS - 1, tile % 4))
        for tile in range(2):
            value = strip_s[series, tile * SLOTS : (tile + 1) * SLOTS, :]
            centres.append(take(value, 3))
            edge = halo[2, series, tile, 0:1, :] * edge_mask[2]
            side_tiles.append(take(value, 4) + edge)
        stage(series, jnp.concatenate(centres, axis=0), side_tiles)
        return carry

    lax.fori_loop(0, SERIES, north_stage, 0)
    filter_across(0)
    lax.fori_loop(0, SERIES, south_stage, 0)
    filter_across(ROWS)

    first_half = lane < 64

    def filter_down(series, tile):
        base = tile * SLOTS
        m = live_mask[...]
        s = [across[series, pl.ds(base + SLOTS * n, SLOTS), :] for n in range(STEP + 4)]
        b = [swapped[series, pl.ds(base + SLOTS * n, SLOTS), :] for n in range(STEP + 4)]
        o = [jnp.where(first_half, b[n], b[n + 1]) for n in range(STEP + 3)]
        for n in range(STEP):
            total = (
                d[0] * s[n + 2] + d[1] * (o[n + 2] + o[n + 1]) + d[2] * (s[n + 3] + s[n + 1])
                + d[3] * (o[n + 3] + o[n]) + d[4] * (s[n + 4] + s[n])
            )
            done[series, pl.ds(base + SLOTS * n, SLOTS), :] = total * m

    def out_copy(chunk):
        span = pl.ds(pl.multiple_of(chunk * (STEP * SLOTS), 8), STEP * SLOTS)
        return pltpu.make_async_copy(
            done.at[:, span, :], out_hbm.at[:, span, :], out_sem.at[chunk]
        )

    def bulk(j, carry):
        y_wait(j + 3)
        first = bulk_row(j)
        for n in range(STEP):
            mix_tile(first + n * SLOTS)

        def stage_step(series, inner):
            side_tiles = [
                own_side(series, first + n * SLOTS, j + (2 + n) // 4, (2 + n) % 4)
                for n in range(STEP)
            ]
            stage(series, mixed[series, pl.ds(first, STEP * SLOTS), :], side_tiles)
            return inner

        def down_step(series, inner):
            filter_down(series, j * STEP)
            return inner

        lax.fori_loop(0, SERIES, stage_step, 0)
        filter_across(first + 2 * SLOTS)
        lax.fori_loop(0, SERIES, down_step, 0)
        out_copy(j).start()
        return carry

    lax.fori_loop(0, CHUNKS, bulk, 0)

    def last_step(series, carry):
        filter_down(series, TILES - STEP)
        return carry

    lax.fori_loop(0, SERIES, last_step, 0)
    out_copy(CHUNKS).start()

    for side, there in ((0, has_right), (1, has_left)):
        @pl.when(there)
        def _(side=side):
            for item in range(3):
                y_copy(side, item).wait_send()

            def sent(j, carry):
                y_copy(side, j).wait_send()
                return carry

            lax.fori_loop(3, 3 + CHUNKS, sent, 0)

    for index, (dx, dz) in enumerate(PLACES):
        @pl.when(place_exists(dx, dz))
        def _(index=index):
            p_copy(index).wait_send()

    for side, there in ((0, has_south), (1, has_north)):
        @pl.when(there)
        def _(side=side):
            z_copy(side).wait_send()

    def written(chunk, carry):
        out_copy(chunk).wait()
        return carry

    lax.fori_loop(0, CHUNKS + 1, written, 0)


def shards(input_field, active_mask, neighbours, time_taps, space_taps, coregion_factor):
    shape = input_field.shape
    tiles = input_field.reshape(2, DAYS, SLOTS, TILES, 128).transpose(0, 1, 3, 2, 4)
    tiles = tiles.reshape(SERIES, ROWS, 128)
    f32 = jnp.float32
    vmem = pltpu.VMEM
    smem = pl.BlockSpec(memory_space=pltpu.SMEM)
    dma = pltpu.SemaphoreType.DMA
    out = pl.pallas_call(
        kernel,
        out_shape=jax.ShapeDtypeStruct((SERIES, ROWS, 128), f32),
        in_specs=[
            pl.BlockSpec(memory_space=pl.ANY),
            pl.BlockSpec(memory_space=pltpu.VMEM),
            smem, smem, smem, smem,
        ],
        out_specs=pl.BlockSpec(memory_space=pl.ANY),
        scratch_shapes=[
            vmem((SERIES, ROWS, 128), f32),
            vmem((SERIES, ROWS, 128), f32),
            vmem((SERIES, ROWS, 128), f32),
            vmem((DAYS * SLOTS, 128), f32),
            vmem((DAYS * SLOTS, 128), f32),
            vmem((DAYS * SLOTS, 128), f32),
            vmem((DAYS * SLOTS, 128), f32),
            vmem((6, DAYS * SLOTS, 128), f32),
            vmem((SERIES, ROWS, 128), f32),
            vmem((SERIES, 16, 128), f32),
            vmem((SERIES, 16, 128), f32),
            vmem((3, SERIES, 4, SLOTS, 128), f32),
            vmem((SERIES * STEP * SLOTS, 768), jnp.bfloat16),
            vmem((768, 256), jnp.bfloat16),
            vmem((SERIES, ROWS + 32, 128), f32),
            vmem((SERIES, ROWS + 32, 128), f32),
            vmem((SERIES, ROWS, 128), f32),
            vmem((5, SLOTS, 128), jnp.int32),
            vmem((5, SLOTS, 128), f32),
            vmem((3, SLOTS, 128), f32),
            vmem((SLOTS, 128), f32),
            dma,
            dma((2, 3 + CHUNKS)),
            dma((2, 3 + CHUNKS)),
            dma((2,)),
            dma((2,)),
            dma((6,)),
            dma((6,)),
            dma((CHUNKS + 1,)),
        ],
        compiler_params=pltpu.CompilerParams(collective_id=0, has_side_effects=True),
    )(tiles, neighbours, active_mask, time_taps, space_taps, coregion_factor)
    out = out.reshape(2, DAYS, TILES, SLOTS, 128).transpose(0, 1, 3, 2, 4)
    return out.reshape(shape)


def solution(mesh):
    in_specs = (P(None, "day", "blk", None), P("blk"), P("blk", None), P(), P(), P())
    out_specs = P(None, "day", "blk", None)
    return jax.shard_map(shards, mesh=mesh, in_specs=in_specs, out_specs=out_specs, check_vma=False)
```

```python
import functools

import jax
import jax.numpy as jnp
from jax import lax
from jax.experimental import pallas as pl
from jax.experimental.pallas import tpu as pltpu
from jax.sharding import PartitionSpec as P

MESH = pl.DeviceIdType.MESH
REACH = 4
SLOTS = 8
DAYS = 3
SERIES = 2 * DAYS
TILES = 32
ROWS = TILES * SLOTS
STEP = 4
CHUNKS = (TILES - 4) // STEP
AHEAD = 1
EARLY = 4
NONE = -(1 << 20)

EAST, WEST, NORTH, SOUTH, NE, NW, SE, SW = range(8)
PLACES = ((1, 0), (-1, 0), (1, -1), (-1, -1), (1, 1), (-1, 1))
OPPOSITE = (1, 0, 5, 4, 3, 2)


def kernel(
    x_hbm, nbr_hbm, act_hbm, time_hbm, space_hbm, factor_hbm, done,
    own, left, right, pack, pack_left, pack_right, pack_mixed, packs,
    mixed, strip_n, strip_s, halo, lhs, weights, across, swapped,
    take_index, take_mask, edge_mask, live_mask,
    nbr, act, time_taps, space_taps, factor,
    load_sem, small_sem, y_send, y_recv, z_send, z_recv, p_send, p_recv,
):
    f32, bf16 = jnp.float32, jnp.bfloat16
    blk, day = lax.axis_index("blk"), lax.axis_index("day")
    blks, days = lax.axis_size("blk"), lax.axis_size("day")
    col, row, rows = blk % REACH, blk // REACH, blks // REACH

    has_left, has_right = day > 0, day < days - 1
    has_north, has_south = row > 0, row < rows - 1

    def place_exists(dx, dz):
        ok = (col + dx >= 0) & (col + dx < REACH)
        if dz:
            ok = ok & (row + dz >= 0) & (row + dz < rows)
        return ok

    partners = [(has_left, 0, -1), (has_right, 0, 1), (has_north, -REACH, 0), (has_south, REACH, 0)]
    for dx, dz in PLACES:
        partners.append((place_exists(dx, dz), dx + REACH * dz, 0))

    barrier = pltpu.get_barrier_semaphore()
    expected = 0
    for there, db, dd in partners:
        @pl.when(there)
        def _(db=db, dd=dd):
            pl.semaphore_signal(
                barrier, inc=1, device_id={"blk": blk + db, "day": day + dd}, device_id_type=MESH
            )
        expected = expected + there.astype(jnp.int32)

    small = [
        pltpu.make_async_copy(source, target, small_sem.at[index])
        for index, (source, target) in enumerate((
            (nbr_hbm, nbr), (act_hbm, act), (time_hbm, time_taps), (space_hbm, space_taps),
            (factor_hbm, factor),
        ))
    ]
    for copy in small:
        copy.start()
    load = pltpu.make_async_copy(x_hbm, own, load_sem)
    load.start()

    pl.semaphore_wait(barrier, expected)

    def bulk_row(j):
        at = 16 + j * (STEP * SLOTS)
        return at if isinstance(j, int) else pl.multiple_of(at, 8)

    def y_copy(side, item):
        target = left if side == 0 else right
        if isinstance(item, int) and item == 0:
            source, target = pack, (pack_left if side == 0 else pack_right)
        else:
            if isinstance(item, int) and item < 3:
                span = pl.ds(0 if item == 1 else ROWS - 16, 16)
            else:
                span = pl.ds(bulk_row(item - 3), STEP * SLOTS)
            source, target = x_hbm.at[:, span, :], target.at[:, span, :]
        return pltpu.make_async_remote_copy(
            src_ref=source, dst_ref=target,
            send_sem=y_send.at[side, item], recv_sem=y_recv.at[side, item],
            device_id={"blk": blk, "day": day + (1 if side == 0 else -1)}, device_id_type=MESH,
        )

    for side, there in ((0, has_right), (1, has_left)):
        @pl.when(there)
        def _(side=side):
            for item in range(1, 3 + AHEAD):
                y_copy(side, item).start()

    for copy in small:
        copy.wait()

    lane = lax.broadcasted_iota(jnp.int32, (SLOTS, 128), 1)
    cell = lane & 63
    low, high = cell < 4, cell >= 60
    slot = lax.broadcasted_iota(jnp.int32, (SLOTS, 128), 0)

    def named(direction):
        column = jnp.broadcast_to(nbr[:, direction : direction + 1], (SLOTS, 128))
        return jnp.where(column < 0, NONE, column)

    def on(target, db):
        first = (blk + db) * SLOTS
        return (target >= first) & (target < first + SLOTS)

    def sides(east, west):
        return jnp.where(low, named(east), jnp.where(high, named(west), NONE))

    for index, (target, db) in enumerate((
        (sides(EAST, WEST), 0),
        (named(NORTH), -REACH), (sides(NE, NW), -REACH),
        (named(SOUTH), REACH), (sides(SE, SW), REACH),
    )):
        take_index[index] = target & (SLOTS - 1)
        take_mask[index] = jnp.where(on(target, db), 1.0, 0.0).astype(f32)
    for index, (east, west, dz) in enumerate(((EAST, WEST, 0), (NE, NW, -1), (SE, SW, 1))):
        there = (low & on(named(east), REACH * dz + 1)) | (high & on(named(west), REACH * dz - 1))
        edge_mask[index] = jnp.where(there, 1.0, 0.0).astype(f32)
    at_east = on(named(EAST), 1) | on(named(NE), 1 - REACH) | on(named(SE), 1 + REACH)
    at_west = on(named(WEST), -1) | on(named(NW), -1 - REACH) | on(named(SW), -1 + REACH)
    ends = jnp.where((high & at_east) | (low & at_west), 1.0, 0.0).astype(f32)
    end_slot = jnp.broadcast_to(
        jnp.sum(ends * slot.astype(f32), axis=0, keepdims=True), (SLOTS, 128)
    ).astype(jnp.int32)
    end_mask = jnp.broadcast_to(jnp.sum(ends, axis=0, keepdims=True), (SLOTS, 128))
    live = jnp.zeros((SLOTS, 128), f32)
    for s in range(SLOTS):
        live = jnp.where(slot == s, act[s].astype(f32), live)
    live_mask[...] = live

    @pl.when(jnp.logical_not(has_left))
    def _():
        pack_left[...] = jnp.zeros_like(pack_left)

        def clear(i, carry):
            left[i] = jnp.zeros((ROWS, 128), f32)
            return carry

        lax.fori_loop(0, SERIES, clear, 0)

    @pl.when(jnp.logical_not(has_right))
    def _():
        pack_right[...] = jnp.zeros_like(pack_right)

        def clear(i, carry):
            right[i] = jnp.zeros((ROWS, 128), f32)
            return carry

        lax.fori_loop(0, SERIES, clear, 0)

    @pl.when(jnp.logical_not(has_north))
    def _():
        strip_n[...] = jnp.zeros_like(strip_n)

    @pl.when(jnp.logical_not(has_south))
    def _():
        strip_s[...] = jnp.zeros_like(strip_s)

    for index, (dx, dz) in enumerate(PLACES):
        @pl.when(jnp.logical_not(place_exists(dx, dz)))
        def _(index=index):
            packs[index] = jnp.zeros((DAYS * SLOTS, 128), f32)

    load.wait()

    for t in range(DAYS):
        total = jnp.zeros((SLOTS, 128), f32)
        for c in range(2):
            for q in range(4):
                part = None
                for g in range(SLOTS):
                    value = own[c * DAYS + t, pl.ds((4 * g + q) * SLOTS, SLOTS), :]
                    value = jnp.take_along_axis(value, end_slot, axis=0)
                    part = value if part is None else jnp.where(slot == g, value, part)
                part = part * end_mask
                shift = 8 * (4 * c + q)
                total = total + (pltpu.roll(part, shift, 1) if shift else part)
        pack[t * SLOTS : (t + 1) * SLOTS, :] = total

    for side, there in ((0, has_right), (1, has_left)):
        @pl.when(there)
        def _(side=side):
            y_copy(side, 0).start()

            def send(j, carry):
                y_copy(side, j).start()
                return carry

            lax.fori_loop(3 + AHEAD, 3 + CHUNKS, send, 0)

    def y_wait(item):
        for side, there in ((0, has_left), (1, has_right)):
            @pl.when(there)
            def _(side=side):
                y_copy(side, item).wait_recv()

    w = [time_taps[k] for k in range(DAYS + 1)]
    a = [space_taps[0, k] for k in range(5)]
    d = [space_taps[1, k] for k in range(5)]
    k00 = factor[0, 0] * factor[0, 0] + factor[0, 1] * factor[0, 1]
    k01 = factor[0, 0] * factor[1, 0] + factor[0, 1] * factor[1, 1]
    k11 = factor[1, 0] * factor[1, 0] + factor[1, 1] * factor[1, 1]

    k = lax.broadcasted_iota(jnp.int32, (256, 256), 0)
    n = lax.broadcasted_iota(jnp.int32, (256, 256), 1)
    place = k & 63
    beyond = jnp.where(place < 4, place + 64, jnp.where(place >= 60, place - 64, 1024))
    place = jnp.where(k >= 128, beyond, place)
    distance = jnp.abs(place - (n & 63))
    same_row = ((k >> 6) & 1) == (((n >> 6) ^ (n >> 7)) & 1)
    weight = jnp.zeros((256, 256), f32)
    for tap in range(5):
        weight = jnp.where(same_row & (distance == tap), a[tap], weight)
    weight_high = weight.astype(bf16)
    weights[0:256, :] = weight_high
    weights[256:512, :] = weight_high
    weights[512:768, :] = (weight - weight_high.astype(f32)).astype(bf16)

    def filtered(v):
        return [
            w[0] * v[t + 3] + w[1] * (v[t + 2] + v[t + 4])
            + w[2] * (v[t + 1] + v[t + 5]) + w[3] * (v[t] + v[t + 6])
            for t in range(DAYS)
        ]

    def mix_tile(at):
        span = pl.ds(at, SLOTS)
        f = []
        for c in range(2):
            v = [ref[c * DAYS + t, span, :] for ref in (left, own, right) for t in range(DAYS)]
            f.append(filtered(v))
        m = live_mask[...]
        for t in range(DAYS):
            mixed[t, span, :] = (k00 * f[0][t] + k01 * f[1][t]) * m
            mixed[DAYS + t, span, :] = (k01 * f[0][t] + k11 * f[1][t]) * m

    for item in range(3):
        y_wait(item)
    v = [
        ref[t * SLOTS : (t + 1) * SLOTS, :]
        for ref in (pack_left, pack, pack_right) for t in range(DAYS)
    ]
    second = (((lane + 68) >> 3) & 7) >= 4
    for t, f in enumerate(filtered(v)):
        first_part = k00 * f + k01 * pltpu.roll(f, 96, 1)
        second_part = k11 * f + k01 * pltpu.roll(f, 32, 1)
        pack_mixed[t * SLOTS : (t + 1) * SLOTS, :] = jnp.where(second, second_part, first_part)
    for tile in (0, 1, TILES - 2, TILES - 1):
        mix_tile(tile * SLOTS)

    def p_copy(index):
        dx, dz = PLACES[index]
        return pltpu.make_async_remote_copy(
            src_ref=pack_mixed, dst_ref=packs.at[OPPOSITE[index]],
            send_sem=p_send.at[index], recv_sem=p_recv.at[OPPOSITE[index]],
            device_id={"blk": blk + dx + REACH * dz, "day": day}, device_id_type=MESH,
        )

    def p_arrival(index):
        return pltpu.make_async_remote_copy(
            src_ref=pack_mixed, dst_ref=packs.at[index],
            send_sem=p_send.at[index], recv_sem=p_recv.at[index],
            device_id={"blk": blk, "day": day}, device_id_type=MESH,
        )

    def z_copy(side):
        span = pl.ds(ROWS - 16, 16) if side == 0 else pl.ds(0, 16)
        return pltpu.make_async_remote_copy(
            src_ref=mixed.at[:, span, :], dst_ref=strip_n if side == 0 else strip_s,
            send_sem=z_send.at[side], recv_sem=z_recv.at[side],
            device_id={"blk": blk + (REACH if side == 0 else -REACH), "day": day},
            device_id_type=MESH,
        )

    for index, (dx, dz) in enumerate(PLACES):
        @pl.when(place_exists(dx, dz))
        def _(index=index):
            p_copy(index).start()

    for side, there in ((0, has_south), (1, has_north)):
        @pl.when(there)
        def _(side=side):
            z_copy(side).start()

    def mix_chunk(j, carry):
        y_wait(j + 3)
        for n in range(STEP):
            mix_tile(bulk_row(j) + n * SLOTS)
        return carry

    lax.fori_loop(0, EARLY, mix_chunk, 0)

    for index, (dx, dz) in enumerate(PLACES):
        @pl.when(place_exists(dx, dz))
        def _(index=index):
            p_arrival(index).wait_recv()

    for side, there in ((0, has_north), (1, has_south)):
        @pl.when(there)
        def _(side=side):
            z_copy(side).wait_recv()

    west_lanes = (lane & 7) < 4
    for t in range(DAYS):
        span = slice(t * SLOTS, (t + 1) * SLOTS)
        for index in range(3):
            both = jnp.where(west_lanes, packs[2 * index, span, :], packs[2 * index + 1, span, :])
            for c in range(2):
                for q in range(4):
                    shift = 8 * (4 * c + q)
                    value = pltpu.roll(both, 128 - shift, 1) if shift else both
                    halo[index, c * DAYS + t, q] = value

    def take(value, index):
        return jnp.take_along_axis(value, take_index[index], axis=0) * take_mask[index]

    def own_side(series, at, g, q):
        side = take(mixed[series, pl.ds(at, SLOTS), :], 0)
        return side + halo[0, series, q, pl.ds(g, 1), :] * edge_mask[0]

    def stage(series, centres, side_tiles):
        span = pl.ds(pl.multiple_of(series * (STEP * SLOTS), 8), STEP * SLOTS)
        for column, value in ((0, centres), (128, jnp.concatenate(side_tiles, axis=0))):
            top = value.astype(bf16)
            rest = (value - top.astype(f32)).astype(bf16)
            lhs[span, column : column + 128] = top
            lhs[span, 256 + column : 384 + column] = rest
            lhs[span, 512 + column : 640 + column] = top

    def filter_across(at):
        result = jnp.dot(lhs[...], weights[...], preferred_element_type=f32)
        for series in range(SERIES):
            part = result[series * STEP * SLOTS : (series + 1) * STEP * SLOTS]
            across[series, pl.ds(at, STEP * SLOTS), :] = part[:, :128]
            swapped[series, pl.ds(at, STEP * SLOTS), :] = part[:, 128:]

    def north_stage(series, carry):
        centres, side_tiles = [], []
        for tile in range(2):
            value = strip_n[series, tile * SLOTS : (tile + 1) * SLOTS, :]
            centres.append(take(value, 1))
            edge = halo[1, series, 2 + tile, SLOTS - 1 : SLOTS, :] * edge_mask[1]
            side_tiles.append(take(value, 2) + edge)
        for tile in range(2):
            centres.append(mixed[series, tile * SLOTS : (tile + 1) * SLOTS, :])
            side_tiles.append(own_side(series, tile * SLOTS, 0, tile))
        stage(series, jnp.concatenate(centres, axis=0), side_tiles)
        return carry

    def south_stage(series, carry):
        centres, side_tiles = [], []
        for tile in range(TILES - 2, TILES):
            centres.append(mixed[series, tile * SLOTS : (tile + 1) * SLOTS, :])
            side_tiles.append(own_side(series, tile * SLOTS, SLOTS - 1, tile % 4))
        for tile in range(2):
            value = strip_s[series, tile * SLOTS : (tile + 1) * SLOTS, :]
            centres.append(take(value, 3))
            edge = halo[2, series, tile, 0:1, :] * edge_mask[2]
            side_tiles.append(take(value, 4) + edge)
        stage(series, jnp.concatenate(centres, axis=0), side_tiles)
        return carry

    lax.fori_loop(0, SERIES, north_stage, 0)
    filter_across(0)
    lax.fori_loop(0, SERIES, south_stage, 0)
    filter_across(ROWS)

    first_half = lane < 64

    def filter_down(series, tile):
        base = tile * SLOTS
        m = live_mask[...]
        s = [across[series, pl.ds(base + SLOTS * n, SLOTS), :] for n in range(STEP + 4)]
        b = [swapped[series, pl.ds(base + SLOTS * n, SLOTS), :] for n in range(STEP + 4)]
        o = [jnp.where(first_half, b[n], b[n + 1]) for n in range(STEP + 3)]
        for n in range(STEP):
            total = (
                d[0] * s[n + 2] + d[1] * (o[n + 2] + o[n + 1]) + d[2] * (s[n + 3] + s[n + 1])
                + d[3] * (o[n + 3] + o[n]) + d[4] * (s[n + 4] + s[n])
            )
            done[series, pl.ds(base + SLOTS * n, SLOTS), :] = total * m

    def space_chunk(j, carry):
        first = bulk_row(j)

        def stage_step(series, inner):
            side_tiles = [
                own_side(series, first + n * SLOTS, j + (2 + n) // 4, (2 + n) % 4)
                for n in range(STEP)
            ]
            stage(series, mixed[series, pl.ds(first, STEP * SLOTS), :], side_tiles)
            return inner

        def down_step(series, inner):
            filter_down(series, j * STEP)
            return inner

        lax.fori_loop(0, SERIES, stage_step, 0)
        filter_across(first + 2 * SLOTS)
        lax.fori_loop(0, SERIES, down_step, 0)
        return carry

    lax.fori_loop(0, EARLY, space_chunk, 0)

    def bulk(j, carry):
        mix_chunk(j, carry)
        return space_chunk(j, carry)

    lax.fori_loop(EARLY, CHUNKS, bulk, 0)

    def last_step(series, carry):
        filter_down(series, TILES - STEP)
        return carry

    lax.fori_loop(0, SERIES, last_step, 0)

    for side, there in ((0, has_right), (1, has_left)):
        @pl.when(there)
        def _(side=side):
            for item in range(3):
                y_copy(side, item).wait_send()

            def sent(j, carry):
                y_copy(side, j).wait_send()
                return carry

            lax.fori_loop(3, 3 + CHUNKS, sent, 0)

    for index, (dx, dz) in enumerate(PLACES):
        @pl.when(place_exists(dx, dz))
        def _(index=index):
            p_copy(index).wait_send()

    for side, there in ((0, has_south), (1, has_north)):
        @pl.when(there)
        def _(side=side):
            z_copy(side).wait_send()


def shards(input_field, active_mask, neighbours, time_taps, space_taps, coregion_factor):
    shape = input_field.shape
    tiles = input_field.reshape(2, DAYS, SLOTS, TILES, 128).transpose(0, 1, 3, 2, 4)
    tiles = tiles.reshape(SERIES, ROWS, 128)
    f32 = jnp.float32
    vmem = pltpu.VMEM
    dma = pltpu.SemaphoreType.DMA
    out = pl.pallas_call(
        kernel,
        out_shape=vmem((SERIES, ROWS, 128), f32),
        in_specs=[pl.BlockSpec(memory_space=pl.ANY)] * 6,
        out_specs=pl.BlockSpec(memory_space=vmem),
        scratch_shapes=[
            vmem((SERIES, ROWS, 128), f32),
            vmem((SERIES, ROWS, 128), f32),
            vmem((SERIES, ROWS, 128), f32),
            vmem((DAYS * SLOTS, 128), f32),
            vmem((DAYS * SLOTS, 128), f32),
            vmem((DAYS * SLOTS, 128), f32),
            vmem((DAYS * SLOTS, 128), f32),
            vmem((6, DAYS * SLOTS, 128), f32),
            vmem((SERIES, ROWS, 128), f32),
            vmem((SERIES, 16, 128), f32),
            vmem((SERIES, 16, 128), f32),
            vmem((3, SERIES, 4, SLOTS, 128), f32),
            vmem((SERIES * STEP * SLOTS, 768), jnp.bfloat16),
            vmem((768, 256), jnp.bfloat16),
            vmem((SERIES, ROWS + 32, 128), f32),
            vmem((SERIES, ROWS + 32, 128), f32),
            vmem((5, SLOTS, 128), jnp.int32),
            vmem((5, SLOTS, 128), f32),
            vmem((3, SLOTS, 128), f32),
            vmem((SLOTS, 128), f32),
            vmem((SLOTS, 8), jnp.int32),
            pltpu.SMEM((SLOTS,), jnp.int32),
            pltpu.SMEM((DAYS + 1,), f32),
            pltpu.SMEM((2, 5), f32),
            pltpu.SMEM((2, 2), f32),
            dma,
            dma((5,)),
            dma((2, 3 + CHUNKS)),
            dma((2, 3 + CHUNKS)),
            dma((2,)),
            dma((2,)),
            dma((6,)),
            dma((6,)),
        ],
        compiler_params=pltpu.CompilerParams(collective_id=0, has_side_effects=True),
    )(tiles, neighbours, active_mask, time_taps, space_taps, coregion_factor)
    out = out.reshape(2, DAYS, TILES, SLOTS, 128).transpose(0, 1, 3, 2, 4)
    return out.reshape(shape)


def solution(mesh):
    in_specs = (P(None, "day", "blk", None), P("blk"), P("blk", None), P(), P(), P())
    out_specs = P(None, "day", "blk", None)
    return jax.shard_map(shards, mesh=mesh, in_specs=in_specs, out_specs=out_specs, check_vma=False)
```

```python
import functools

import jax
import jax.numpy as jnp
from jax import lax
from jax.experimental import pallas as pl
from jax.experimental.pallas import tpu as pltpu
from jax.sharding import PartitionSpec as P

MESH = pl.DeviceIdType.MESH
REACH = 4
SLOTS = 8
DAYS = 3
SERIES = 2 * DAYS
TILES = 32
ROWS = TILES * SLOTS
STEP = 4
CHUNKS = (TILES - 4) // STEP
AHEAD = 0
EARLY = 3
NONE = -(1 << 20)

EAST, WEST, NORTH, SOUTH, NE, NW, SE, SW = range(8)
PLACES = ((1, 0), (-1, 0), (1, -1), (-1, -1), (1, 1), (-1, 1))
OPPOSITE = (1, 0, 5, 4, 3, 2)


def kernel(
    x_hbm, nbr_hbm, act_hbm, time_hbm, space_hbm, factor_hbm, done,
    own, left, right, pack, pack_left, pack_right, pack_mixed, packs,
    mixed, strip_n, strip_s, halo, lhs, weights, across, swapped,
    take_index, take_mask, edge_mask, live_mask,
    nbr, act, time_taps, space_taps, factor,
    load_sem, small_sem, y_send, y_recv, z_send, z_recv, p_send, p_recv,
    days_ready, edges_ready,
):
    f32, bf16 = jnp.float32, jnp.bfloat16
    blk, day = lax.axis_index("blk"), lax.axis_index("day")
    blks, days = lax.axis_size("blk"), lax.axis_size("day")
    col, row, rows = blk % REACH, blk // REACH, blks // REACH

    has_left, has_right = day > 0, day < days - 1
    has_north, has_south = row > 0, row < rows - 1

    def place_exists(dx, dz):
        ok = (col + dx >= 0) & (col + dx < REACH)
        if dz:
            ok = ok & (row + dz >= 0) & (row + dz < rows)
        return ok

    core = day % 2
    chip = day - core
    first_core, second_core = core == 0, core == 1
    barrier = pltpu.get_barrier_semaphore()

    def hello(there, db, to_day):
        @pl.when(there)
        def _():
            pl.semaphore_signal(
                barrier, inc=1, device_id={"blk": blk + db, "day": to_day}, device_id_type=MESH
            )

    def tell(sem, to_day):
        pl.semaphore_signal(
            sem, inc=1, device_id={"blk": blk, "day": to_day}, device_id_type=MESH
        )

    hello(first_core, 0, day + 1)
    hello(first_core & has_left, 0, day - 1)
    hello(second_core & has_right, 0, day + 2)
    expected_days = 1 + has_right.astype(jnp.int32) + (day > 1).astype(jnp.int32)
    expected_edges = 0
    for there, db in [(has_north, -REACH), (has_south, REACH)] + [
        (place_exists(dx, dz), dx + REACH * dz) for dx, dz in PLACES
    ]:
        hello(there, db, chip)
        expected_edges = expected_edges + 2 * there.astype(jnp.int32)

    small = [
        pltpu.make_async_copy(source, target, small_sem.at[index])
        for index, (source, target) in enumerate((
            (nbr_hbm, nbr), (act_hbm, act), (time_hbm, time_taps), (space_hbm, space_taps),
            (factor_hbm, factor),
        ))
    ]
    for copy in small:
        copy.start()
    load = pltpu.make_async_copy(x_hbm, own, load_sem)
    load.start()

    @pl.when(second_core)
    def _():
        pl.semaphore_wait(barrier, expected_days)
        tell(days_ready, day - 1)

    @pl.when(first_core)
    def _():
        pl.semaphore_wait(days_ready, 1)

    def bulk_row(j):
        at = 16 + j * (STEP * SLOTS)
        return at if isinstance(j, int) else pl.multiple_of(at, 8)

    def y_copy(side, item):
        target = left if side == 0 else right
        if isinstance(item, int) and item == 0:
            source, target = pack, (pack_left if side == 0 else pack_right)
        else:
            if isinstance(item, int) and item < 3:
                span = pl.ds(0 if item == 1 else ROWS - 16, 16)
            else:
                span = pl.ds(bulk_row(item - 3), STEP * SLOTS)
            source, target = x_hbm.at[:, span, :], target.at[:, span, :]
        return pltpu.make_async_remote_copy(
            src_ref=source, dst_ref=target,
            send_sem=y_send.at[side, item], recv_sem=y_recv.at[side, item],
            device_id={"blk": blk, "day": day + (1 if side == 0 else -1)}, device_id_type=MESH,
        )

    for side, there in ((0, has_right), (1, has_left)):
        @pl.when(there)
        def _(side=side):
            for item in range(1, 3 + AHEAD):
                y_copy(side, item).start()

    for copy in small:
        copy.wait()

    lane = lax.broadcasted_iota(jnp.int32, (SLOTS, 128), 1)
    cell = lane & 63
    low, high = cell < 4, cell >= 60
    slot = lax.broadcasted_iota(jnp.int32, (SLOTS, 128), 0)

    def named(direction):
        column = jnp.broadcast_to(nbr[:, direction : direction + 1], (SLOTS, 128))
        return jnp.where(column < 0, NONE, column)

    def on(target, db):
        first = (blk + db) * SLOTS
        return (target >= first) & (target < first + SLOTS)

    def sides(east, west):
        return jnp.where(low, named(east), jnp.where(high, named(west), NONE))

    for index, (target, db) in enumerate((
        (sides(EAST, WEST), 0),
        (named(NORTH), -REACH), (sides(NE, NW), -REACH),
        (named(SOUTH), REACH), (sides(SE, SW), REACH),
    )):
        take_index[index] = target & (SLOTS - 1)
        take_mask[index] = jnp.where(on(target, db), 1.0, 0.0).astype(f32)
    for index, (east, west, dz) in enumerate(((EAST, WEST, 0), (NE, NW, -1), (SE, SW, 1))):
        there = (low & on(named(east), REACH * dz + 1)) | (high & on(named(west), REACH * dz - 1))
        edge_mask[index] = jnp.where(there, 1.0, 0.0).astype(f32)
    at_east = on(named(EAST), 1) | on(named(NE), 1 - REACH) | on(named(SE), 1 + REACH)
    at_west = on(named(WEST), -1) | on(named(NW), -1 - REACH) | on(named(SW), -1 + REACH)
    ends = jnp.where((high & at_east) | (low & at_west), 1.0, 0.0).astype(f32)
    end_slot = jnp.broadcast_to(
        jnp.sum(ends * slot.astype(f32), axis=0, keepdims=True), (SLOTS, 128)
    ).astype(jnp.int32)
    end_mask = jnp.broadcast_to(jnp.sum(ends, axis=0, keepdims=True), (SLOTS, 128))
    live = jnp.zeros((SLOTS, 128), f32)
    for s in range(SLOTS):
        live = jnp.where(slot == s, act[s].astype(f32), live)
    live_mask[...] = live

    @pl.when(jnp.logical_not(has_left))
    def _():
        pack_left[...] = jnp.zeros_like(pack_left)

        def clear(i, carry):
            left[i] = jnp.zeros((ROWS, 128), f32)
            return carry

        lax.fori_loop(0, SERIES, clear, 0)

    @pl.when(jnp.logical_not(has_right))
    def _():
        pack_right[...] = jnp.zeros_like(pack_right)

        def clear(i, carry):
            right[i] = jnp.zeros((ROWS, 128), f32)
            return carry

        lax.fori_loop(0, SERIES, clear, 0)

    @pl.when(jnp.logical_not(has_north))
    def _():
        strip_n[...] = jnp.zeros_like(strip_n)

    @pl.when(jnp.logical_not(has_south))
    def _():
        strip_s[...] = jnp.zeros_like(strip_s)

    for index, (dx, dz) in enumerate(PLACES):
        @pl.when(jnp.logical_not(place_exists(dx, dz)))
        def _(index=index):
            packs[index] = jnp.zeros((DAYS * SLOTS, 128), f32)

    load.wait()

    for t in range(DAYS):
        total = jnp.zeros((SLOTS, 128), f32)
        for c in range(2):
            for q in range(4):
                part = None
                for g in range(SLOTS):
                    value = own[c * DAYS + t, pl.ds((4 * g + q) * SLOTS, SLOTS), :]
                    value = jnp.take_along_axis(value, end_slot, axis=0)
                    part = value if part is None else jnp.where(slot == g, value, part)
                part = part * end_mask
                shift = 8 * (4 * c + q)
                total = total + (pltpu.roll(part, shift, 1) if shift else part)
        pack[t * SLOTS : (t + 1) * SLOTS, :] = total

    for side, there in ((0, has_right), (1, has_left)):
        @pl.when(there)
        def _(side=side):
            y_copy(side, 0).start()

            def send(j, carry):
                y_copy(side, j).start()
                return carry

            lax.fori_loop(3 + AHEAD, 3 + CHUNKS, send, 0)

    def y_wait(item):
        for side, there in ((0, has_left), (1, has_right)):
            @pl.when(there)
            def _(side=side):
                y_copy(side, item).wait_recv()

    w = [time_taps[k] for k in range(DAYS + 1)]
    a = [space_taps[0, k] for k in range(5)]
    d = [space_taps[1, k] for k in range(5)]
    k00 = factor[0, 0] * factor[0, 0] + factor[0, 1] * factor[0, 1]
    k01 = factor[0, 0] * factor[1, 0] + factor[0, 1] * factor[1, 1]
    k11 = factor[1, 0] * factor[1, 0] + factor[1, 1] * factor[1, 1]

    k = lax.broadcasted_iota(jnp.int32, (256, 256), 0)
    n = lax.broadcasted_iota(jnp.int32, (256, 256), 1)
    place = k & 63
    beyond = jnp.where(place < 4, place + 64, jnp.where(place >= 60, place - 64, 1024))
    place = jnp.where(k >= 128, beyond, place)
    distance = jnp.abs(place - (n & 63))
    same_row = ((k >> 6) & 1) == (((n >> 6) ^ (n >> 7)) & 1)
    weight = jnp.zeros((256, 256), f32)
    for tap in range(5):
        weight = jnp.where(same_row & (distance == tap), a[tap], weight)
    weight_high = weight.astype(bf16)
    weights[0:256, :] = weight_high
    weights[256:512, :] = weight_high
    weights[512:768, :] = (weight - weight_high.astype(f32)).astype(bf16)

    def filtered(v):
        return [
            w[0] * v[t + 3] + w[1] * (v[t + 2] + v[t + 4])
            + w[2] * (v[t + 1] + v[t + 5]) + w[3] * (v[t] + v[t + 6])
            for t in range(DAYS)
        ]

    def mix_tile(at):
        span = pl.ds(at, SLOTS)
        f = []
        for c in range(2):
            v = [ref[c * DAYS + t, span, :] for ref in (left, own, right) for t in range(DAYS)]
            f.append(filtered(v))
        m = live_mask[...]
        for t in range(DAYS):
            mixed[t, span, :] = (k00 * f[0][t] + k01 * f[1][t]) * m
            mixed[DAYS + t, span, :] = (k01 * f[0][t] + k11 * f[1][t]) * m

    for item in range(3):
        y_wait(item)
    v = [
        ref[t * SLOTS : (t + 1) * SLOTS, :]
        for ref in (pack_left, pack, pack_right) for t in range(DAYS)
    ]
    second = (((lane + 68) >> 3) & 7) >= 4
    for t, f in enumerate(filtered(v)):
        first_part = k00 * f + k01 * pltpu.roll(f, 96, 1)
        second_part = k11 * f + k01 * pltpu.roll(f, 32, 1)
        pack_mixed[t * SLOTS : (t + 1) * SLOTS, :] = jnp.where(second, second_part, first_part)
    for tile in (0, 1, TILES - 2, TILES - 1):
        mix_tile(tile * SLOTS)

    def p_copy(index):
        dx, dz = PLACES[index]
        return pltpu.make_async_remote_copy(
            src_ref=pack_mixed, dst_ref=packs.at[OPPOSITE[index]],
            send_sem=p_send.at[index], recv_sem=p_recv.at[OPPOSITE[index]],
            device_id={"blk": blk + dx + REACH * dz, "day": day}, device_id_type=MESH,
        )

    def p_arrival(index):
        return pltpu.make_async_remote_copy(
            src_ref=pack_mixed, dst_ref=packs.at[index],
            send_sem=p_send.at[index], recv_sem=p_recv.at[index],
            device_id={"blk": blk, "day": day}, device_id_type=MESH,
        )

    def z_copy(side):
        span = pl.ds(ROWS - 16, 16) if side == 0 else pl.ds(0, 16)
        return pltpu.make_async_remote_copy(
            src_ref=mixed.at[:, span, :], dst_ref=strip_n if side == 0 else strip_s,
            send_sem=z_send.at[side], recv_sem=z_recv.at[side],
            device_id={"blk": blk + (REACH if side == 0 else -REACH), "day": day},
            device_id_type=MESH,
        )

    @pl.when(first_core)
    def _():
        pl.semaphore_wait(barrier, expected_edges)
        tell(edges_ready, day + 1)

    @pl.when(second_core)
    def _():
        pl.semaphore_wait(edges_ready, 1)

    for index, (dx, dz) in enumerate(PLACES):
        @pl.when(place_exists(dx, dz))
        def _(index=index):
            p_copy(index).start()

    for side, there in ((0, has_south), (1, has_north)):
        @pl.when(there)
        def _(side=side):
            z_copy(side).start()

    def mix_chunk(j, carry):
        y_wait(j + 3)
        for n in range(STEP):
            mix_tile(bulk_row(j) + n * SLOTS)
        return carry

    lax.fori_loop(0, EARLY, mix_chunk, 0)

    for index, (dx, dz) in enumerate(PLACES):
        @pl.when(place_exists(dx, dz))
        def _(index=index):
            p_arrival(index).wait_recv()

    for side, there in ((0, has_north), (1, has_south)):
        @pl.when(there)
        def _(side=side):
            z_copy(side).wait_recv()

    west_lanes = (lane & 7) < 4
    for t in range(DAYS):
        span = slice(t * SLOTS, (t + 1) * SLOTS)
        for index in range(3):
            both = jnp.where(west_lanes, packs[2 * index, span, :], packs[2 * index + 1, span, :])
            for c in range(2):
                for q in range(4):
                    shift = 8 * (4 * c + q)
                    value = pltpu.roll(both, 128 - shift, 1) if shift else both
                    halo[index, c * DAYS + t, q] = value

    def take(value, index):
        return jnp.take_along_axis(value, take_index[index], axis=0) * take_mask[index]

    def own_side(series, at, g, q):
        side = take(mixed[series, pl.ds(at, SLOTS), :], 0)
        return side + halo[0, series, q, pl.ds(g, 1), :] * edge_mask[0]

    def stage(series, centres, side_tiles):
        span = pl.ds(pl.multiple_of(series * (STEP * SLOTS), 8), STEP * SLOTS)
        for column, value in ((0, centres), (128, jnp.concatenate(side_tiles, axis=0))):
            top = value.astype(bf16)
            rest = (value - top.astype(f32)).astype(bf16)
            lhs[span, column : column + 128] = top
            lhs[span, 256 + column : 384 + column] = rest
            lhs[span, 512 + column : 640 + column] = top

    def filter_across(at):
        result = jnp.dot(lhs[...], weights[...], preferred_element_type=f32)
        for series in range(SERIES):
            part = result[series * STEP * SLOTS : (series + 1) * STEP * SLOTS]
            across[series, pl.ds(at, STEP * SLOTS), :] = part[:, :128]
            swapped[series, pl.ds(at, STEP * SLOTS), :] = part[:, 128:]

    def north_stage(series, carry):
        centres, side_tiles = [], []
        for tile in range(2):
            value = strip_n[series, tile * SLOTS : (tile + 1) * SLOTS, :]
            centres.append(take(value, 1))
            edge = halo[1, series, 2 + tile, SLOTS - 1 : SLOTS, :] * edge_mask[1]
            side_tiles.append(take(value, 2) + edge)
        for tile in range(2):
            centres.append(mixed[series, tile * SLOTS : (tile + 1) * SLOTS, :])
            side_tiles.append(own_side(series, tile * SLOTS, 0, tile))
        stage(series, jnp.concatenate(centres, axis=0), side_tiles)
        return carry

    def south_stage(series, carry):
        centres, side_tiles = [], []
        for tile in range(TILES - 2, TILES):
            centres.append(mixed[series, tile * SLOTS : (tile + 1) * SLOTS, :])
            side_tiles.append(own_side(series, tile * SLOTS, SLOTS - 1, tile % 4))
        for tile in range(2):
            value = strip_s[series, tile * SLOTS : (tile + 1) * SLOTS, :]
            centres.append(take(value, 3))
            edge = halo[2, series, tile, 0:1, :] * edge_mask[2]
            side_tiles.append(take(value, 4) + edge)
        stage(series, jnp.concatenate(centres, axis=0), side_tiles)
        return carry

    lax.fori_loop(0, SERIES, north_stage, 0)
    filter_across(0)
    lax.fori_loop(0, SERIES, south_stage, 0)
    filter_across(ROWS)

    first_half = lane < 64

    def filter_down(series, tile):
        base = tile * SLOTS
        m = live_mask[...]
        s = [across[series, pl.ds(base + SLOTS * n, SLOTS), :] for n in range(STEP + 4)]
        b = [swapped[series, pl.ds(base + SLOTS * n, SLOTS), :] for n in range(STEP + 4)]
        o = [jnp.where(first_half, b[n], b[n + 1]) for n in range(STEP + 3)]
        for n in range(STEP):
            total = (
                d[0] * s[n + 2] + d[1] * (o[n + 2] + o[n + 1]) + d[2] * (s[n + 3] + s[n + 1])
                + d[3] * (o[n + 3] + o[n]) + d[4] * (s[n + 4] + s[n])
            )
            done[series, pl.ds(base + SLOTS * n, SLOTS), :] = total * m

    def space_chunk(j, carry):
        first = bulk_row(j)

        def stage_step(series, inner):
            side_tiles = [
                own_side(series, first + n * SLOTS, j + (2 + n) // 4, (2 + n) % 4)
                for n in range(STEP)
            ]
            stage(series, mixed[series, pl.ds(first, STEP * SLOTS), :], side_tiles)
            return inner

        def down_step(series, inner):
            filter_down(series, j * STEP)
            return inner

        lax.fori_loop(0, SERIES, stage_step, 0)
        filter_across(first + 2 * SLOTS)
        lax.fori_loop(0, SERIES, down_step, 0)
        return carry

    lax.fori_loop(0, EARLY, space_chunk, 0)

    def bulk(j, carry):
        mix_chunk(j, carry)
        return space_chunk(j, carry)

    lax.fori_loop(EARLY, CHUNKS, bulk, 0)

    def last_step(series, carry):
        filter_down(series, TILES - STEP)
        return carry

    lax.fori_loop(0, SERIES, last_step, 0)

    for side, there in ((0, has_right), (1, has_left)):
        @pl.when(there)
        def _(side=side):
            for item in range(3):
                y_copy(side, item).wait_send()

            def sent(j, carry):
                y_copy(side, j).wait_send()
                return carry

            lax.fori_loop(3, 3 + CHUNKS, sent, 0)

    for index, (dx, dz) in enumerate(PLACES):
        @pl.when(place_exists(dx, dz))
        def _(index=index):
            p_copy(index).wait_send()

    for side, there in ((0, has_south), (1, has_north)):
        @pl.when(there)
        def _(side=side):
            z_copy(side).wait_send()


def shards(input_field, active_mask, neighbours, time_taps, space_taps, coregion_factor):
    shape = input_field.shape
    tiles = input_field.reshape(2, DAYS, SLOTS, TILES, 128).transpose(0, 1, 3, 2, 4)
    tiles = tiles.reshape(SERIES, ROWS, 128)
    f32 = jnp.float32
    vmem = pltpu.VMEM
    dma = pltpu.SemaphoreType.DMA
    out = pl.pallas_call(
        kernel,
        out_shape=vmem((SERIES, ROWS, 128), f32),
        in_specs=[pl.BlockSpec(memory_space=pl.ANY)] * 6,
        out_specs=pl.BlockSpec(memory_space=vmem),
        scratch_shapes=[
            vmem((SERIES, ROWS, 128), f32),
            vmem((SERIES, ROWS, 128), f32),
            vmem((SERIES, ROWS, 128), f32),
            vmem((DAYS * SLOTS, 128), f32),
            vmem((DAYS * SLOTS, 128), f32),
            vmem((DAYS * SLOTS, 128), f32),
            vmem((DAYS * SLOTS, 128), f32),
            vmem((6, DAYS * SLOTS, 128), f32),
            vmem((SERIES, ROWS, 128), f32),
            vmem((SERIES, 16, 128), f32),
            vmem((SERIES, 16, 128), f32),
            vmem((3, SERIES, 4, SLOTS, 128), f32),
            vmem((SERIES * STEP * SLOTS, 768), jnp.bfloat16),
            vmem((768, 256), jnp.bfloat16),
            vmem((SERIES, ROWS + 32, 128), f32),
            vmem((SERIES, ROWS + 32, 128), f32),
            vmem((5, SLOTS, 128), jnp.int32),
            vmem((5, SLOTS, 128), f32),
            vmem((3, SLOTS, 128), f32),
            vmem((SLOTS, 128), f32),
            vmem((SLOTS, 8), jnp.int32),
            pltpu.SMEM((SLOTS,), jnp.int32),
            pltpu.SMEM((DAYS + 1,), f32),
            pltpu.SMEM((2, 5), f32),
            pltpu.SMEM((2, 2), f32),
            dma,
            dma((5,)),
            dma((2, 3 + CHUNKS)),
            dma((2, 3 + CHUNKS)),
            dma((2,)),
            dma((2,)),
            dma((6,)),
            dma((6,)),
            pltpu.SemaphoreType.REGULAR,
            pltpu.SemaphoreType.REGULAR,
        ],
        compiler_params=pltpu.CompilerParams(collective_id=0, has_side_effects=True),
    )(tiles, neighbours, active_mask, time_taps, space_taps, coregion_factor)
    out = out.reshape(2, DAYS, TILES, SLOTS, 128).transpose(0, 1, 3, 2, 4)
    return out.reshape(shape)


def solution(mesh):
    in_specs = (P(None, "day", "blk", None), P("blk"), P("blk", None), P(), P(), P())
    out_specs = P(None, "day", "blk", None)
    return jax.shard_map(shards, mesh=mesh, in_specs=in_specs, out_specs=out_specs, check_vma=False)
```

```python
import functools

import jax
import jax.numpy as jnp
from jax import lax
from jax.experimental import pallas as pl
from jax.experimental.pallas import tpu as pltpu
from jax.sharding import PartitionSpec as P

MESH = pl.DeviceIdType.MESH
REACH = 4
SLOTS = 8
DAYS = 3
SERIES = 2 * DAYS
TILES = 32
ROWS = TILES * SLOTS
STEP = 4
CHUNKS = (TILES - 4) // STEP
AHEAD = 0
EARLY = 3
NONE = -(1 << 20)

EAST, WEST, NORTH, SOUTH, NE, NW, SE, SW = range(8)
PLACES = ((1, 0), (-1, 0), (1, -1), (-1, -1), (1, 1), (-1, 1))
OPPOSITE = (1, 0, 5, 4, 3, 2)


def kernel(
    x_hbm, nbr_hbm, act_hbm, time_hbm, space_hbm, factor_hbm, done,
    own, left, right, pack, pack_left, pack_right, pack_mixed, packs,
    mixed, strip_n, strip_s, halo, lhs, weights, across, swapped,
    take_index, take_mask, edge_mask, live_mask,
    nbr, act, time_taps, space_taps, factor,
    load_sem, small_sem, y_send, y_recv, z_send, z_recv, p_send, p_recv,
    days_ready, edges_ready,
):
    f32, bf16 = jnp.float32, jnp.bfloat16
    blk, day = lax.axis_index("blk"), lax.axis_index("day")
    blks, days = lax.axis_size("blk"), lax.axis_size("day")
    col, row, rows = blk % REACH, blk // REACH, blks // REACH

    has_left, has_right = day > 0, day < days - 1
    has_north, has_south = row > 0, row < rows - 1

    def place_exists(dx, dz):
        ok = (col + dx >= 0) & (col + dx < REACH)
        if dz:
            ok = ok & (row + dz >= 0) & (row + dz < rows)
        return ok

    core = day % 2
    chip = day - core
    first_core, second_core = core == 0, core == 1
    barrier = pltpu.get_barrier_semaphore()

    def hello(there, db, to_day):
        @pl.when(there)
        def _():
            pl.semaphore_signal(
                barrier, inc=1, device_id={"blk": blk + db, "day": to_day}, device_id_type=MESH
            )

    def tell(sem, to_day):
        pl.semaphore_signal(
            sem, inc=1, device_id={"blk": blk, "day": to_day}, device_id_type=MESH
        )

    first_chip = day < 2
    hello(first_core & ~first_chip, 0, day + 1)
    hello(first_core & has_left, 0, day - 1)
    hello(second_core & has_right, 0, day + 2)
    hello(second_core & first_chip, 0, day - 1)
    expected_days = has_right.astype(jnp.int32) + 2 * (day > 1).astype(jnp.int32)
    expected_edges = first_chip.astype(jnp.int32)
    for there, db in [(has_north, -REACH), (has_south, REACH)] + [
        (place_exists(dx, dz), dx + REACH * dz) for dx, dz in PLACES
    ]:
        hello(there, db, chip)
        expected_edges = expected_edges + 2 * there.astype(jnp.int32)

    small = [
        pltpu.make_async_copy(source, target, small_sem.at[index])
        for index, (source, target) in enumerate((
            (nbr_hbm, nbr), (act_hbm, act), (time_hbm, time_taps), (space_hbm, space_taps),
            (factor_hbm, factor),
        ))
    ]
    for copy in small:
        copy.start()
    load = pltpu.make_async_copy(x_hbm, own, load_sem)
    load.start()

    @pl.when(second_core)
    def _():
        pl.semaphore_wait(barrier, expected_days)

    @pl.when(second_core & ~first_chip)
    def _():
        tell(days_ready, day - 1)

    @pl.when(first_core & ~first_chip)
    def _():
        pl.semaphore_wait(days_ready, 1)

    def edges_entered():
        pl.semaphore_wait(barrier, expected_edges)
        tell(edges_ready, day + 1)

    @pl.when(first_core & first_chip)
    def _():
        edges_entered()

    def bulk_row(j):
        at = 16 + j * (STEP * SLOTS)
        return at if isinstance(j, int) else pl.multiple_of(at, 8)

    def y_copy(side, item):
        target = left if side == 0 else right
        if isinstance(item, int) and item == 0:
            source, target = pack, (pack_left if side == 0 else pack_right)
        else:
            if isinstance(item, int) and item < 3:
                span = pl.ds(0 if item == 1 else ROWS - 16, 16)
            else:
                span = pl.ds(bulk_row(item - 3), STEP * SLOTS)
            source, target = x_hbm.at[:, span, :], target.at[:, span, :]
        return pltpu.make_async_remote_copy(
            src_ref=source, dst_ref=target,
            send_sem=y_send.at[side, item], recv_sem=y_recv.at[side, item],
            device_id={"blk": blk, "day": day + (1 if side == 0 else -1)}, device_id_type=MESH,
        )

    for side, there in ((0, has_right), (1, day > 1)):
        @pl.when(there)
        def _(side=side):
            for item in range(1, 3 + AHEAD):
                y_copy(side, item).start()

    for copy in small:
        copy.wait()

    lane = lax.broadcasted_iota(jnp.int32, (SLOTS, 128), 1)
    cell = lane & 63
    low, high = cell < 4, cell >= 60
    slot = lax.broadcasted_iota(jnp.int32, (SLOTS, 128), 0)

    def named(direction):
        column = jnp.broadcast_to(nbr[:, direction : direction + 1], (SLOTS, 128))
        return jnp.where(column < 0, NONE, column)

    def on(target, db):
        first = (blk + db) * SLOTS
        return (target >= first) & (target < first + SLOTS)

    def sides(east, west):
        return jnp.where(low, named(east), jnp.where(high, named(west), NONE))

    for index, (target, db) in enumerate((
        (sides(EAST, WEST), 0),
        (named(NORTH), -REACH), (sides(NE, NW), -REACH),
        (named(SOUTH), REACH), (sides(SE, SW), REACH),
    )):
        take_index[index] = target & (SLOTS - 1)
        take_mask[index] = jnp.where(on(target, db), 1.0, 0.0).astype(f32)
    for index, (east, west, dz) in enumerate(((EAST, WEST, 0), (NE, NW, -1), (SE, SW, 1))):
        there = (low & on(named(east), REACH * dz + 1)) | (high & on(named(west), REACH * dz - 1))
        edge_mask[index] = jnp.where(there, 1.0, 0.0).astype(f32)
    at_east = on(named(EAST), 1) | on(named(NE), 1 - REACH) | on(named(SE), 1 + REACH)
    at_west = on(named(WEST), -1) | on(named(NW), -1 - REACH) | on(named(SW), -1 + REACH)
    ends = jnp.where((high & at_east) | (low & at_west), 1.0, 0.0).astype(f32)
    end_slot = jnp.broadcast_to(
        jnp.sum(ends * slot.astype(f32), axis=0, keepdims=True), (SLOTS, 128)
    ).astype(jnp.int32)
    end_mask = jnp.broadcast_to(jnp.sum(ends, axis=0, keepdims=True), (SLOTS, 128))
    live = jnp.zeros((SLOTS, 128), f32)
    for s in range(SLOTS):
        live = jnp.where(slot == s, act[s].astype(f32), live)
    live_mask[...] = live

    @pl.when(jnp.logical_not(has_left))
    def _():
        pack_left[...] = jnp.zeros_like(pack_left)

        def clear(i, carry):
            left[i] = jnp.zeros((ROWS, 128), f32)
            return carry

        lax.fori_loop(0, SERIES, clear, 0)

    @pl.when(jnp.logical_not(has_right))
    def _():
        pack_right[...] = jnp.zeros_like(pack_right)

        def clear(i, carry):
            right[i] = jnp.zeros((ROWS, 128), f32)
            return carry

        lax.fori_loop(0, SERIES, clear, 0)

    @pl.when(jnp.logical_not(has_north))
    def _():
        strip_n[...] = jnp.zeros_like(strip_n)

    @pl.when(jnp.logical_not(has_south))
    def _():
        strip_s[...] = jnp.zeros_like(strip_s)

    for index, (dx, dz) in enumerate(PLACES):
        @pl.when(jnp.logical_not(place_exists(dx, dz)))
        def _(index=index):
            packs[index] = jnp.zeros((DAYS * SLOTS, 128), f32)

    load.wait()

    for t in range(DAYS):
        total = jnp.zeros((SLOTS, 128), f32)
        for c in range(2):
            for q in range(4):
                part = None
                for g in range(SLOTS):
                    value = own[c * DAYS + t, pl.ds((4 * g + q) * SLOTS, SLOTS), :]
                    value = jnp.take_along_axis(value, end_slot, axis=0)
                    part = value if part is None else jnp.where(slot == g, value, part)
                part = part * end_mask
                shift = 8 * (4 * c + q)
                total = total + (pltpu.roll(part, shift, 1) if shift else part)
        pack[t * SLOTS : (t + 1) * SLOTS, :] = total

    def send_rest(side):
        y_copy(side, 0).start()

        def send(j, carry):
            y_copy(side, j).start()
            return carry

        lax.fori_loop(3 + AHEAD, 3 + CHUNKS, send, 0)

    for side, there in ((0, has_right), (1, day > 1)):
        @pl.when(there)
        def _(side=side):
            send_rest(side)

    @pl.when(second_core & first_chip)
    def _():
        pl.semaphore_wait(edges_ready, 1)
        for item in range(1, 3 + AHEAD):
            y_copy(1, item).start()
        send_rest(1)

    def y_wait(item):
        for side, there in ((0, has_left), (1, has_right)):
            @pl.when(there)
            def _(side=side):
                y_copy(side, item).wait_recv()

    w = [time_taps[k] for k in range(DAYS + 1)]
    a = [space_taps[0, k] for k in range(5)]
    d = [space_taps[1, k] for k in range(5)]
    k00 = factor[0, 0] * factor[0, 0] + factor[0, 1] * factor[0, 1]
    k01 = factor[0, 0] * factor[1, 0] + factor[0, 1] * factor[1, 1]
    k11 = factor[1, 0] * factor[1, 0] + factor[1, 1] * factor[1, 1]

    k = lax.broadcasted_iota(jnp.int32, (256, 256), 0)
    n = lax.broadcasted_iota(jnp.int32, (256, 256), 1)
    place = k & 63
    beyond = jnp.where(place < 4, place + 64, jnp.where(place >= 60, place - 64, 1024))
    place = jnp.where(k >= 128, beyond, place)
    distance = jnp.abs(place - (n & 63))
    same_row = ((k >> 6) & 1) == (((n >> 6) ^ (n >> 7)) & 1)
    weight = jnp.zeros((256, 256), f32)
    for tap in range(5):
        weight = jnp.where(same_row & (distance == tap), a[tap], weight)
    weight_high = weight.astype(bf16)
    weights[0:256, :] = weight_high
    weights[256:512, :] = weight_high
    weights[512:768, :] = (weight - weight_high.astype(f32)).astype(bf16)

    def filtered(v):
        return [
            w[0] * v[t + 3] + w[1] * (v[t + 2] + v[t + 4])
            + w[2] * (v[t + 1] + v[t + 5]) + w[3] * (v[t] + v[t + 6])
            for t in range(DAYS)
        ]

    def mix_tile(at):
        span = pl.ds(at, SLOTS)
        f = []
        for c in range(2):
            v = [ref[c * DAYS + t, span, :] for ref in (left, own, right) for t in range(DAYS)]
            f.append(filtered(v))
        m = live_mask[...]
        for t in range(DAYS):
            mixed[t, span, :] = (k00 * f[0][t] + k01 * f[1][t]) * m
            mixed[DAYS + t, span, :] = (k01 * f[0][t] + k11 * f[1][t]) * m

    for item in range(3):
        y_wait(item)
    v = [
        ref[t * SLOTS : (t + 1) * SLOTS, :]
        for ref in (pack_left, pack, pack_right) for t in range(DAYS)
    ]
    second = (((lane + 68) >> 3) & 7) >= 4
    for t, f in enumerate(filtered(v)):
        first_part = k00 * f + k01 * pltpu.roll(f, 96, 1)
        second_part = k11 * f + k01 * pltpu.roll(f, 32, 1)
        pack_mixed[t * SLOTS : (t + 1) * SLOTS, :] = jnp.where(second, second_part, first_part)
    for tile in (0, 1, TILES - 2, TILES - 1):
        mix_tile(tile * SLOTS)

    def p_copy(index):
        dx, dz = PLACES[index]
        return pltpu.make_async_remote_copy(
            src_ref=pack_mixed, dst_ref=packs.at[OPPOSITE[index]],
            send_sem=p_send.at[index], recv_sem=p_recv.at[OPPOSITE[index]],
            device_id={"blk": blk + dx + REACH * dz, "day": day}, device_id_type=MESH,
        )

    def p_arrival(index):
        return pltpu.make_async_remote_copy(
            src_ref=pack_mixed, dst_ref=packs.at[index],
            send_sem=p_send.at[index], recv_sem=p_recv.at[index],
            device_id={"blk": blk, "day": day}, device_id_type=MESH,
        )

    def z_copy(side):
        span = pl.ds(ROWS - 16, 16) if side == 0 else pl.ds(0, 16)
        return pltpu.make_async_remote_copy(
            src_ref=mixed.at[:, span, :], dst_ref=strip_n if side == 0 else strip_s,
            send_sem=z_send.at[side], recv_sem=z_recv.at[side],
            device_id={"blk": blk + (REACH if side == 0 else -REACH), "day": day},
            device_id_type=MESH,
        )

    @pl.when(first_core & ~first_chip)
    def _():
        edges_entered()

    @pl.when(second_core & ~first_chip)
    def _():
        pl.semaphore_wait(edges_ready, 1)

    for index, (dx, dz) in enumerate(PLACES):
        @pl.when(place_exists(dx, dz))
        def _(index=index):
            p_copy(index).start()

    for side, there in ((0, has_south), (1, has_north)):
        @pl.when(there)
        def _(side=side):
            z_copy(side).start()

    def mix_chunk(j, carry):
        y_wait(j + 3)
        for n in range(STEP):
            mix_tile(bulk_row(j) + n * SLOTS)
        return carry

    lax.fori_loop(0, EARLY, mix_chunk, 0)

    for index, (dx, dz) in enumerate(PLACES):
        @pl.when(place_exists(dx, dz))
        def _(index=index):
            p_arrival(index).wait_recv()

    for side, there in ((0, has_north), (1, has_south)):
        @pl.when(there)
        def _(side=side):
            z_copy(side).wait_recv()

    west_lanes = (lane & 7) < 4
    for t in range(DAYS):
        span = slice(t * SLOTS, (t + 1) * SLOTS)
        for index in range(3):
            both = jnp.where(west_lanes, packs[2 * index, span, :], packs[2 * index + 1, span, :])
            for c in range(2):
                for q in range(4):
                    shift = 8 * (4 * c + q)
                    value = pltpu.roll(both, 128 - shift, 1) if shift else both
                    halo[index, c * DAYS + t, q] = value

    def take(value, index):
        return jnp.take_along_axis(value, take_index[index], axis=0) * take_mask[index]

    def own_side(series, at, g, q):
        side = take(mixed[series, pl.ds(at, SLOTS), :], 0)
        return side + halo[0, series, q, pl.ds(g, 1), :] * edge_mask[0]

    def stage(series, centres, side_tiles):
        span = pl.ds(pl.multiple_of(series * (STEP * SLOTS), 8), STEP * SLOTS)
        for column, value in ((0, centres), (128, jnp.concatenate(side_tiles, axis=0))):
            top = value.astype(bf16)
            rest = (value - top.astype(f32)).astype(bf16)
            lhs[span, column : column + 128] = top
            lhs[span, 256 + column : 384 + column] = rest
            lhs[span, 512 + column : 640 + column] = top

    def filter_across(at):
        result = jnp.dot(lhs[...], weights[...], preferred_element_type=f32)
        for series in range(SERIES):
            part = result[series * STEP * SLOTS : (series + 1) * STEP * SLOTS]
            across[series, pl.ds(at, STEP * SLOTS), :] = part[:, :128]
            swapped[series, pl.ds(at, STEP * SLOTS), :] = part[:, 128:]

    def north_stage(series, carry):
        centres, side_tiles = [], []
        for tile in range(2):
            value = strip_n[series, tile * SLOTS : (tile + 1) * SLOTS, :]
            centres.append(take(value, 1))
            edge = halo[1, series, 2 + tile, SLOTS - 1 : SLOTS, :] * edge_mask[1]
            side_tiles.append(take(value, 2) + edge)
        for tile in range(2):
            centres.append(mixed[series, tile * SLOTS : (tile + 1) * SLOTS, :])
            side_tiles.append(own_side(series, tile * SLOTS, 0, tile))
        stage(series, jnp.concatenate(centres, axis=0), side_tiles)
        return carry

    def south_stage(series, carry):
        centres, side_tiles = [], []
        for tile in range(TILES - 2, TILES):
            centres.append(mixed[series, tile * SLOTS : (tile + 1) * SLOTS, :])
            side_tiles.append(own_side(series, tile * SLOTS, SLOTS - 1, tile % 4))
        for tile in range(2):
            value = strip_s[series, tile * SLOTS : (tile + 1) * SLOTS, :]
            centres.append(take(value, 3))
            edge = halo[2, series, tile, 0:1, :] * edge_mask[2]
            side_tiles.append(take(value, 4) + edge)
        stage(series, jnp.concatenate(centres, axis=0), side_tiles)
        return carry

    lax.fori_loop(0, SERIES, north_stage, 0)
    filter_across(0)
    lax.fori_loop(0, SERIES, south_stage, 0)
    filter_across(ROWS)

    first_half = lane < 64

    def filter_down(series, tile):
        base = tile * SLOTS
        m = live_mask[...]
        s = [across[series, pl.ds(base + SLOTS * n, SLOTS), :] for n in range(STEP + 4)]
        b = [swapped[series, pl.ds(base + SLOTS * n, SLOTS), :] for n in range(STEP + 4)]
        o = [jnp.where(first_half, b[n], b[n + 1]) for n in range(STEP + 3)]
        for n in range(STEP):
            total = (
                d[0] * s[n + 2] + d[1] * (o[n + 2] + o[n + 1]) + d[2] * (s[n + 3] + s[n + 1])
                + d[3] * (o[n + 3] + o[n]) + d[4] * (s[n + 4] + s[n])
            )
            done[series, pl.ds(base + SLOTS * n, SLOTS), :] = total * m

    def space_chunk(j, carry):
        first = bulk_row(j)

        def stage_step(series, inner):
            side_tiles = [
                own_side(series, first + n * SLOTS, j + (2 + n) // 4, (2 + n) % 4)
                for n in range(STEP)
            ]
            stage(series, mixed[series, pl.ds(first, STEP * SLOTS), :], side_tiles)
            return inner

        def down_step(series, inner):
            filter_down(series, j * STEP)
            return inner

        lax.fori_loop(0, SERIES, stage_step, 0)
        filter_across(first + 2 * SLOTS)
        lax.fori_loop(0, SERIES, down_step, 0)
        return carry

    lax.fori_loop(0, EARLY, space_chunk, 0)

    def bulk(j, carry):
        mix_chunk(j, carry)
        return space_chunk(j, carry)

    lax.fori_loop(EARLY, CHUNKS, bulk, 0)

    def last_step(series, carry):
        filter_down(series, TILES - STEP)
        return carry

    lax.fori_loop(0, SERIES, last_step, 0)

    for side, there in ((0, has_right), (1, has_left)):
        @pl.when(there)
        def _(side=side):
            for item in range(3):
                y_copy(side, item).wait_send()

            def sent(j, carry):
                y_copy(side, j).wait_send()
                return carry

            lax.fori_loop(3, 3 + CHUNKS, sent, 0)

    for index, (dx, dz) in enumerate(PLACES):
        @pl.when(place_exists(dx, dz))
        def _(index=index):
            p_copy(index).wait_send()

    for side, there in ((0, has_south), (1, has_north)):
        @pl.when(there)
        def _(side=side):
            z_copy(side).wait_send()


def shards(input_field, active_mask, neighbours, time_taps, space_taps, coregion_factor):
    shape = input_field.shape
    tiles = input_field.reshape(2, DAYS, SLOTS, TILES, 128).transpose(0, 1, 3, 2, 4)
    tiles = tiles.reshape(SERIES, ROWS, 128)
    f32 = jnp.float32
    vmem = pltpu.VMEM
    dma = pltpu.SemaphoreType.DMA
    out = pl.pallas_call(
        kernel,
        out_shape=vmem((SERIES, ROWS, 128), f32),
        in_specs=[pl.BlockSpec(memory_space=pl.ANY)] * 6,
        out_specs=pl.BlockSpec(memory_space=vmem),
        scratch_shapes=[
            vmem((SERIES, ROWS, 128), f32),
            vmem((SERIES, ROWS, 128), f32),
            vmem((SERIES, ROWS, 128), f32),
            vmem((DAYS * SLOTS, 128), f32),
            vmem((DAYS * SLOTS, 128), f32),
            vmem((DAYS * SLOTS, 128), f32),
            vmem((DAYS * SLOTS, 128), f32),
            vmem((6, DAYS * SLOTS, 128), f32),
            vmem((SERIES, ROWS, 128), f32),
            vmem((SERIES, 16, 128), f32),
            vmem((SERIES, 16, 128), f32),
            vmem((3, SERIES, 4, SLOTS, 128), f32),
            vmem((SERIES * STEP * SLOTS, 768), jnp.bfloat16),
            vmem((768, 256), jnp.bfloat16),
            vmem((SERIES, ROWS + 32, 128), f32),
            vmem((SERIES, ROWS + 32, 128), f32),
            vmem((5, SLOTS, 128), jnp.int32),
            vmem((5, SLOTS, 128), f32),
            vmem((3, SLOTS, 128), f32),
            vmem((SLOTS, 128), f32),
            vmem((SLOTS, 8), jnp.int32),
            pltpu.SMEM((SLOTS,), jnp.int32),
            pltpu.SMEM((DAYS + 1,), f32),
            pltpu.SMEM((2, 5), f32),
            pltpu.SMEM((2, 2), f32),
            dma,
            dma((5,)),
            dma((2, 3 + CHUNKS)),
            dma((2, 3 + CHUNKS)),
            dma((2,)),
            dma((2,)),
            dma((6,)),
            dma((6,)),
            pltpu.SemaphoreType.REGULAR,
            pltpu.SemaphoreType.REGULAR,
        ],
        compiler_params=pltpu.CompilerParams(collective_id=0, has_side_effects=True),
    )(tiles, neighbours, active_mask, time_taps, space_taps, coregion_factor)
    out = out.reshape(2, DAYS, TILES, SLOTS, 128).transpose(0, 1, 3, 2, 4)
    return out.reshape(shape)


def solution(mesh):
    in_specs = (P(None, "day", "blk", None), P("blk"), P("blk", None), P(), P(), P())
    out_specs = P(None, "day", "blk", None)
    return jax.shard_map(shards, mesh=mesh, in_specs=in_specs, out_specs=out_specs, check_vma=False)
```

```python
import functools

import jax
import jax.numpy as jnp
from jax import lax
from jax.experimental import pallas as pl
from jax.experimental.pallas import tpu as pltpu
from jax.sharding import PartitionSpec as P

MESH = pl.DeviceIdType.MESH
REACH = 4
SLOTS = 8
DAYS = 3
SERIES = 2 * DAYS
TILES = 32
ROWS = TILES * SLOTS
STEP = 4
CHUNKS = (TILES - 4) // STEP
AHEAD = 0
EARLY = 4
NONE = -(1 << 20)

EAST, WEST, NORTH, SOUTH, NE, NW, SE, SW = range(8)
PLACES = ((1, 0), (-1, 0), (1, -1), (-1, -1), (1, 1), (-1, 1))
OPPOSITE = (1, 0, 5, 4, 3, 2)


def kernel(
    x_hbm, nbr_hbm, act_hbm, time_hbm, space_hbm, factor_hbm, done,
    own, left, right, pack, pack_left, pack_right, pack_mixed, packs,
    mixed, strip_n, strip_s, halo, lhs, weights, side_lhs, side_weights, fix, across, swapped,
    take_index, take_mask, edge_mask, fix_mask, live_mask,
    nbr, act, time_taps, space_taps, factor,
    load_sem, small_sem, y_send, y_recv, z_send, z_recv, p_send, p_recv,
    days_ready, edges_ready,
):
    f32, bf16 = jnp.float32, jnp.bfloat16
    blk, day = lax.axis_index("blk"), lax.axis_index("day")
    blks, days = lax.axis_size("blk"), lax.axis_size("day")
    col, row, rows = blk % REACH, blk // REACH, blks // REACH

    has_left, has_right = day > 0, day < days - 1
    has_north, has_south = row > 0, row < rows - 1

    def place_exists(dx, dz):
        ok = (col + dx >= 0) & (col + dx < REACH)
        if dz:
            ok = ok & (row + dz >= 0) & (row + dz < rows)
        return ok

    core = day % 2
    chip = day - core
    first_core, second_core = core == 0, core == 1
    barrier = pltpu.get_barrier_semaphore()

    def hello(there, db, to_day):
        @pl.when(there)
        def _():
            pl.semaphore_signal(
                barrier, inc=1, device_id={"blk": blk + db, "day": to_day}, device_id_type=MESH
            )

    def tell(sem, to_day):
        pl.semaphore_signal(
            sem, inc=1, device_id={"blk": blk, "day": to_day}, device_id_type=MESH
        )

    first_chip = day < 2
    hello(first_core & ~first_chip, 0, day + 1)
    hello(first_core & has_left, 0, day - 1)
    hello(second_core & has_right, 0, day + 2)
    hello(second_core & first_chip, 0, day - 1)
    expected_days = has_right.astype(jnp.int32) + 2 * (day > 1).astype(jnp.int32)
    expected_edges = first_chip.astype(jnp.int32)
    for there, db in [(has_north, -REACH), (has_south, REACH)] + [
        (place_exists(dx, dz), dx + REACH * dz) for dx, dz in PLACES
    ]:
        hello(there, db, chip)
        expected_edges = expected_edges + 2 * there.astype(jnp.int32)

    small = [
        pltpu.make_async_copy(source, target, small_sem.at[index])
        for index, (source, target) in enumerate((
            (nbr_hbm, nbr), (act_hbm, act), (time_hbm, time_taps), (space_hbm, space_taps),
            (factor_hbm, factor),
        ))
    ]
    for copy in small:
        copy.start()
    load = pltpu.make_async_copy(x_hbm, own, load_sem)
    load.start()

    @pl.when(second_core)
    def _():
        pl.semaphore_wait(barrier, expected_days)

    @pl.when(second_core & ~first_chip)
    def _():
        tell(days_ready, day - 1)

    @pl.when(first_core & ~first_chip)
    def _():
        pl.semaphore_wait(days_ready, 1)

    def edges_entered():
        pl.semaphore_wait(barrier, expected_edges)
        tell(edges_ready, day + 1)

    @pl.when(first_core & first_chip)
    def _():
        edges_entered()

    def bulk_row(j):
        at = 16 + j * (STEP * SLOTS)
        return at if isinstance(j, int) else pl.multiple_of(at, 8)

    def y_copy(side, item):
        target = left if side == 0 else right
        if isinstance(item, int) and item == 0:
            source, target = pack, (pack_left if side == 0 else pack_right)
        else:
            if isinstance(item, int) and item < 3:
                span = pl.ds(0 if item == 1 else ROWS - 16, 16)
            else:
                span = pl.ds(bulk_row(item - 3), STEP * SLOTS)
            source, target = x_hbm.at[:, span, :], target.at[:, span, :]
        return pltpu.make_async_remote_copy(
            src_ref=source, dst_ref=target,
            send_sem=y_send.at[side, item], recv_sem=y_recv.at[side, item],
            device_id={"blk": blk, "day": day + (1 if side == 0 else -1)}, device_id_type=MESH,
        )

    for side, there in ((0, has_right), (1, day > 1)):
        @pl.when(there)
        def _(side=side):
            for item in range(1, 3 + AHEAD):
                y_copy(side, item).start()

    for copy in small:
        copy.wait()

    lane = lax.broadcasted_iota(jnp.int32, (SLOTS, 128), 1)
    cell = lane & 63
    low, high = cell < 4, cell >= 60
    slot = lax.broadcasted_iota(jnp.int32, (SLOTS, 128), 0)

    def named(direction):
        column = jnp.broadcast_to(nbr[:, direction : direction + 1], (SLOTS, 128))
        return jnp.where(column < 0, NONE, column)

    def on(target, db):
        first = (blk + db) * SLOTS
        return (target >= first) & (target < first + SLOTS)

    def sides(east, west):
        return jnp.where(low, named(east), jnp.where(high, named(west), NONE))

    for index, (target, db) in enumerate((
        (sides(EAST, WEST), 0),
        (named(NORTH), -REACH), (sides(NE, NW), -REACH),
        (named(SOUTH), REACH), (sides(SE, SW), REACH),
    )):
        take_index[index] = target & (SLOTS - 1)
        take_mask[index] = jnp.where(on(target, db), 1.0, 0.0).astype(f32)
    for index, (east, west, dz) in enumerate(((EAST, WEST, 0), (NE, NW, -1), (SE, SW, 1))):
        there = (low & on(named(east), REACH * dz + 1)) | (high & on(named(west), REACH * dz - 1))
        edge_mask[index] = jnp.where(there, 1.0, 0.0).astype(f32)
    there = (high & on(named(EAST), 1)) | (low & on(named(WEST), -1))
    fix_mask[...] = jnp.where(there, 1.0, 0.0).astype(f32)
    at_east = on(named(EAST), 1) | on(named(NE), 1 - REACH) | on(named(SE), 1 + REACH)
    at_west = on(named(WEST), -1) | on(named(NW), -1 - REACH) | on(named(SW), -1 + REACH)
    ends = jnp.where((high & at_east) | (low & at_west), 1.0, 0.0).astype(f32)
    end_slot = jnp.broadcast_to(
        jnp.sum(ends * slot.astype(f32), axis=0, keepdims=True), (SLOTS, 128)
    ).astype(jnp.int32)
    end_mask = jnp.broadcast_to(jnp.sum(ends, axis=0, keepdims=True), (SLOTS, 128))
    live = jnp.zeros((SLOTS, 128), f32)
    for s in range(SLOTS):
        live = jnp.where(slot == s, act[s].astype(f32), live)
    live_mask[...] = live

    @pl.when(jnp.logical_not(has_left))
    def _():
        pack_left[...] = jnp.zeros_like(pack_left)

        def clear(i, carry):
            left[i] = jnp.zeros((ROWS, 128), f32)
            return carry

        lax.fori_loop(0, SERIES, clear, 0)

    @pl.when(jnp.logical_not(has_right))
    def _():
        pack_right[...] = jnp.zeros_like(pack_right)

        def clear(i, carry):
            right[i] = jnp.zeros((ROWS, 128), f32)
            return carry

        lax.fori_loop(0, SERIES, clear, 0)

    @pl.when(jnp.logical_not(has_north))
    def _():
        strip_n[...] = jnp.zeros_like(strip_n)

    @pl.when(jnp.logical_not(has_south))
    def _():
        strip_s[...] = jnp.zeros_like(strip_s)

    for index, (dx, dz) in enumerate(PLACES):
        @pl.when(jnp.logical_not(place_exists(dx, dz)))
        def _(index=index):
            packs[index] = jnp.zeros((DAYS * SLOTS, 128), f32)

    load.wait()

    for t in range(DAYS):
        total = jnp.zeros((SLOTS, 128), f32)
        for c in range(2):
            for q in range(4):
                part = None
                for g in range(SLOTS):
                    value = own[c * DAYS + t, pl.ds((4 * g + q) * SLOTS, SLOTS), :]
                    value = jnp.take_along_axis(value, end_slot, axis=0)
                    part = value if part is None else jnp.where(slot == g, value, part)
                part = part * end_mask
                shift = 8 * (4 * c + q)
                total = total + (pltpu.roll(part, shift, 1) if shift else part)
        pack[t * SLOTS : (t + 1) * SLOTS, :] = total

    def send_rest(side):
        y_copy(side, 0).start()

        def send(j, carry):
            y_copy(side, j).start()
            return carry

        lax.fori_loop(3 + AHEAD, 3 + CHUNKS, send, 0)

    for side, there in ((0, has_right), (1, day > 1)):
        @pl.when(there)
        def _(side=side):
            send_rest(side)

    @pl.when(second_core & first_chip)
    def _():
        pl.semaphore_wait(edges_ready, 1)
        for item in range(1, 3 + AHEAD):
            y_copy(1, item).start()
        send_rest(1)

    def y_wait(item):
        for side, there in ((0, has_left), (1, has_right)):
            @pl.when(there)
            def _(side=side):
                y_copy(side, item).wait_recv()

    w = [time_taps[k] for k in range(DAYS + 1)]
    a = [space_taps[0, k] for k in range(5)]
    d = [space_taps[1, k] for k in range(5)]
    k00 = factor[0, 0] * factor[0, 0] + factor[0, 1] * factor[0, 1]
    k01 = factor[0, 0] * factor[1, 0] + factor[0, 1] * factor[1, 1]
    k11 = factor[1, 0] * factor[1, 0] + factor[1, 1] * factor[1, 1]

    k = lax.broadcasted_iota(jnp.int32, (256, 256), 0)
    n = lax.broadcasted_iota(jnp.int32, (256, 256), 1)
    place = k & 63
    beyond = jnp.where(place < 4, place + 64, jnp.where(place >= 60, place - 64, 1024))
    place = jnp.where(k >= 128, beyond, place)
    distance = jnp.abs(place - (n & 63))
    same_row = ((k >> 6) & 1) == (((n >> 6) ^ (n >> 7)) & 1)
    weight = jnp.zeros((256, 256), f32)
    for tap in range(5):
        weight = jnp.where(same_row & (distance == tap), a[tap], weight)
    weight_high = weight.astype(bf16)
    weights[0:256, :] = weight_high
    weights[256:512, :] = weight_high
    weight_low = (weight - weight_high.astype(f32)).astype(bf16)
    weights[512:768, :] = weight_low
    side_weights[0:128, :] = weight_high[128:]
    side_weights[128:256, :] = weight_high[128:]
    side_weights[256:384, :] = weight_low[128:]

    def filtered(v):
        return [
            w[0] * v[t + 3] + w[1] * (v[t + 2] + v[t + 4])
            + w[2] * (v[t + 1] + v[t + 5]) + w[3] * (v[t] + v[t + 6])
            for t in range(DAYS)
        ]

    def mix_tile(at):
        span = pl.ds(at, SLOTS)
        f = []
        for c in range(2):
            v = [ref[c * DAYS + t, span, :] for ref in (left, own, right) for t in range(DAYS)]
            f.append(filtered(v))
        m = live_mask[...]
        for t in range(DAYS):
            mixed[t, span, :] = (k00 * f[0][t] + k01 * f[1][t]) * m
            mixed[DAYS + t, span, :] = (k01 * f[0][t] + k11 * f[1][t]) * m

    for item in range(3):
        y_wait(item)
    v = [
        ref[t * SLOTS : (t + 1) * SLOTS, :]
        for ref in (pack_left, pack, pack_right) for t in range(DAYS)
    ]
    second = (((lane + 68) >> 3) & 7) >= 4
    for t, f in enumerate(filtered(v)):
        first_part = k00 * f + k01 * pltpu.roll(f, 96, 1)
        second_part = k11 * f + k01 * pltpu.roll(f, 32, 1)
        pack_mixed[t * SLOTS : (t + 1) * SLOTS, :] = jnp.where(second, second_part, first_part)
    for tile in (0, 1, TILES - 2, TILES - 1):
        mix_tile(tile * SLOTS)

    def p_copy(index):
        dx, dz = PLACES[index]
        return pltpu.make_async_remote_copy(
            src_ref=pack_mixed, dst_ref=packs.at[OPPOSITE[index]],
            send_sem=p_send.at[index], recv_sem=p_recv.at[OPPOSITE[index]],
            device_id={"blk": blk + dx + REACH * dz, "day": day}, device_id_type=MESH,
        )

    def p_arrival(index):
        return pltpu.make_async_remote_copy(
            src_ref=pack_mixed, dst_ref=packs.at[index],
            send_sem=p_send.at[index], recv_sem=p_recv.at[index],
            device_id={"blk": blk, "day": day}, device_id_type=MESH,
        )

    def z_copy(side):
        span = pl.ds(ROWS - 16, 16) if side == 0 else pl.ds(0, 16)
        return pltpu.make_async_remote_copy(
            src_ref=mixed.at[:, span, :], dst_ref=strip_n if side == 0 else strip_s,
            send_sem=z_send.at[side], recv_sem=z_recv.at[side],
            device_id={"blk": blk + (REACH if side == 0 else -REACH), "day": day},
            device_id_type=MESH,
        )

    @pl.when(first_core & ~first_chip)
    def _():
        edges_entered()

    @pl.when(second_core & ~first_chip)
    def _():
        pl.semaphore_wait(edges_ready, 1)

    for index, (dx, dz) in enumerate(PLACES):
        @pl.when(place_exists(dx, dz))
        def _(index=index):
            p_copy(index).start()

    for side, there in ((0, has_south), (1, has_north)):
        @pl.when(there)
        def _(side=side):
            z_copy(side).start()

    def take(value, index):
        return jnp.take_along_axis(value, take_index[index], axis=0) * take_mask[index]

    def own_side(series, at):
        return take(mixed[series, pl.ds(at, SLOTS), :], 0)

    def split(value):
        top = value.astype(bf16)
        return top, (value - top.astype(f32)).astype(bf16)

    def stage(series, centres, side_tiles):
        span = pl.ds(pl.multiple_of(series * (STEP * SLOTS), 8), STEP * SLOTS)
        for column, value in ((0, centres), (128, jnp.concatenate(side_tiles, axis=0))):
            top, rest = split(value)
            lhs[span, column : column + 128] = top
            lhs[span, 256 + column : 384 + column] = rest
            lhs[span, 512 + column : 640 + column] = top

    def filter_across(first_at, second_at):
        result = jnp.dot(lhs[...], weights[...], preferred_element_type=f32)
        half = STEP * SLOTS // 2
        for series in range(SERIES):
            for at, row in ((first_at, 2 * series), (second_at, 2 * series + 1)):
                part = result[row * half : (row + 1) * half]
                across[series, pl.ds(at, half), :] = part[:, :128]
                swapped[series, pl.ds(at, half), :] = part[:, 128:]

    def across_chunk(j, sides_of):
        first = bulk_row(j)

        def stage_step(series, inner):
            side_tiles = [sides_of(series, first + n * SLOTS, n) for n in range(STEP)]
            stage(series, mixed[series, pl.ds(first, STEP * SLOTS), :], side_tiles)
            return inner

        lax.fori_loop(0, SERIES, stage_step, 0)
        filter_across(first + 16, first + 32)

    def rim_stage(series, carry):
        spots = [tile * SLOTS for tile in (0, 1, TILES - 2, TILES - 1)]
        centres = [mixed[series, at : at + SLOTS, :] for at in spots]
        stage(series, jnp.concatenate(centres, axis=0), [own_side(series, at) for at in spots])
        return carry

    lax.fori_loop(0, SERIES, rim_stage, 0)
    filter_across(16, ROWS)

    def mix_chunk(j, carry):
        y_wait(j + 3)
        for n in range(STEP):
            mix_tile(bulk_row(j) + n * SLOTS)
        return carry

    def early_chunk(j, carry):
        mix_chunk(j, carry)
        across_chunk(j, lambda series, at, n: own_side(series, at))
        return carry

    lax.fori_loop(0, EARLY, early_chunk, 0)

    for index, (dx, dz) in enumerate(PLACES):
        @pl.when(place_exists(dx, dz))
        def _(index=index):
            p_arrival(index).wait_recv()

    for side, there in ((0, has_north), (1, has_south)):
        @pl.when(there)
        def _(side=side):
            z_copy(side).wait_recv()

    west_lanes = (lane & 7) < 4
    for t in range(DAYS):
        span = slice(t * SLOTS, (t + 1) * SLOTS)
        for index in range(3):
            both = jnp.where(west_lanes, packs[2 * index, span, :], packs[2 * index + 1, span, :])
            for c in range(2):
                for q in range(4):
                    shift = 8 * (4 * c + q)
                    value = pltpu.roll(both, 128 - shift, 1) if shift else both
                    halo[index, c * DAYS + t, q] = value

    def side_stage(series, carry):
        span = pl.ds(pl.multiple_of(series * (4 * SLOTS), 8), 4 * SLOTS)
        value = jnp.concatenate([halo[0, series, q] for q in range(4)], axis=0)
        top, rest = split(value)
        side_lhs[span, 0:128] = top
        side_lhs[span, 128:256] = rest
        side_lhs[span, 256:384] = top
        return carry

    lax.fori_loop(0, SERIES, side_stage, 0)
    added = jnp.dot(side_lhs[...], side_weights[...], preferred_element_type=f32)
    fix[0] = added[:, :128]
    fix[1] = added[:, 128:]

    def outer_stage(series, carry):
        centres, side_tiles = [], []
        for strip, index, edge, tiles, g in (
            (strip_n, 1, 1, (2, 3), SLOTS - 1), (strip_s, 3, 2, (0, 1), 0)
        ):
            for n, q in enumerate(tiles):
                value = strip[series, n * SLOTS : (n + 1) * SLOTS, :]
                centres.append(take(value, index))
                side = halo[edge, series, q, g : g + 1, :] * edge_mask[edge]
                side_tiles.append(take(value, index + 1) + side)
        stage(series, jnp.concatenate(centres, axis=0), side_tiles)
        return carry

    lax.fori_loop(0, SERIES, outer_stage, 0)
    filter_across(0, ROWS + 16)

    def add_fix(series, at, g, q):
        row = (series * 4 + q) * SLOTS + g
        span = pl.ds(at + 2 * SLOTS, SLOTS)
        m = fix_mask[...]
        across[series, span, :] = across[series, span, :] + fix[0, pl.ds(row, 1), :] * m
        swapped[series, span, :] = swapped[series, span, :] + fix[1, pl.ds(row, 1), :] * m

    def rim_fix(series, carry):
        for tile in (0, 1, TILES - 2, TILES - 1):
            add_fix(series, tile * SLOTS, tile // 4, tile % 4)
        return carry

    lax.fori_loop(0, SERIES, rim_fix, 0)

    first_half = lane < 64

    def filter_down(series, tile):
        base = tile * SLOTS
        m = live_mask[...]
        s = [across[series, pl.ds(base + SLOTS * n, SLOTS), :] for n in range(STEP + 4)]
        b = [swapped[series, pl.ds(base + SLOTS * n, SLOTS), :] for n in range(STEP + 4)]
        o = [jnp.where(first_half, b[n], b[n + 1]) for n in range(STEP + 3)]
        for n in range(STEP):
            total = (
                d[0] * s[n + 2] + d[1] * (o[n + 2] + o[n + 1]) + d[2] * (s[n + 3] + s[n + 1])
                + d[3] * (o[n + 3] + o[n]) + d[4] * (s[n + 4] + s[n])
            )
            done[series, pl.ds(base + SLOTS * n, SLOTS), :] = total * m

    def late_down(j, carry):
        def down_step(series, inner):
            filter_down(series, j * STEP)
            return inner

        return lax.fori_loop(0, SERIES, down_step, carry)

    def fixed_down(j, carry):
        first = bulk_row(j)

        def down_step(series, inner):
            for n in range(STEP):
                add_fix(series, first + n * SLOTS, j + (2 + n) // 4, (2 + n) % 4)
            filter_down(series, j * STEP)
            return inner

        return lax.fori_loop(0, SERIES, down_step, carry)

    lax.fori_loop(0, EARLY, fixed_down, 0)

    def bulk(j, carry):
        mix_chunk(j, carry)

        def sides_of(series, at, n):
            row = halo[0, series, (2 + n) % 4, pl.ds(j + (2 + n) // 4, 1), :]
            return own_side(series, at) + row * edge_mask[0]

        across_chunk(j, sides_of)
        return late_down(j, carry)

    lax.fori_loop(EARLY, CHUNKS, bulk, 0)

    def last_step(series, carry):
        filter_down(series, TILES - STEP)
        return carry

    lax.fori_loop(0, SERIES, last_step, 0)

    for side, there in ((0, has_right), (1, has_left)):
        @pl.when(there)
        def _(side=side):
            for item in range(3):
                y_copy(side, item).wait_send()

            def sent(j, carry):
                y_copy(side, j).wait_send()
                return carry

            lax.fori_loop(3, 3 + CHUNKS, sent, 0)

    for index, (dx, dz) in enumerate(PLACES):
        @pl.when(place_exists(dx, dz))
        def _(index=index):
            p_copy(index).wait_send()

    for side, there in ((0, has_south), (1, has_north)):
        @pl.when(there)
        def _(side=side):
            z_copy(side).wait_send()


def shards(input_field, active_mask, neighbours, time_taps, space_taps, coregion_factor):
    shape = input_field.shape
    tiles = input_field.reshape(2, DAYS, SLOTS, TILES, 128).transpose(0, 1, 3, 2, 4)
    tiles = tiles.reshape(SERIES, ROWS, 128)
    f32 = jnp.float32
    vmem = pltpu.VMEM
    dma = pltpu.SemaphoreType.DMA
    out = pl.pallas_call(
        kernel,
        out_shape=vmem((SERIES, ROWS, 128), f32),
        in_specs=[pl.BlockSpec(memory_space=pl.ANY)] * 6,
        out_specs=pl.BlockSpec(memory_space=vmem),
        scratch_shapes=[
            vmem((SERIES, ROWS, 128), f32),
            vmem((SERIES, ROWS, 128), f32),
            vmem((SERIES, ROWS, 128), f32),
            vmem((DAYS * SLOTS, 128), f32),
            vmem((DAYS * SLOTS, 128), f32),
            vmem((DAYS * SLOTS, 128), f32),
            vmem((DAYS * SLOTS, 128), f32),
            vmem((6, DAYS * SLOTS, 128), f32),
            vmem((SERIES, ROWS, 128), f32),
            vmem((SERIES, 16, 128), f32),
            vmem((SERIES, 16, 128), f32),
            vmem((3, SERIES, 4, SLOTS, 128), f32),
            vmem((SERIES * STEP * SLOTS, 768), jnp.bfloat16),
            vmem((768, 256), jnp.bfloat16),
            vmem((SERIES * 4 * SLOTS, 384), jnp.bfloat16),
            vmem((384, 256), jnp.bfloat16),
            vmem((2, SERIES * 4 * SLOTS, 128), f32),
            vmem((SERIES, ROWS + 32, 128), f32),
            vmem((SERIES, ROWS + 32, 128), f32),
            vmem((5, SLOTS, 128), jnp.int32),
            vmem((5, SLOTS, 128), f32),
            vmem((3, SLOTS, 128), f32),
            vmem((SLOTS, 128), f32),
            vmem((SLOTS, 128), f32),
            vmem((SLOTS, 8), jnp.int32),
            pltpu.SMEM((SLOTS,), jnp.int32),
            pltpu.SMEM((DAYS + 1,), f32),
            pltpu.SMEM((2, 5), f32),
            pltpu.SMEM((2, 2), f32),
            dma,
            dma((5,)),
            dma((2, 3 + CHUNKS)),
            dma((2, 3 + CHUNKS)),
            dma((2,)),
            dma((2,)),
            dma((6,)),
            dma((6,)),
            pltpu.SemaphoreType.REGULAR,
            pltpu.SemaphoreType.REGULAR,
        ],
        compiler_params=pltpu.CompilerParams(collective_id=0, has_side_effects=True),
    )(tiles, neighbours, active_mask, time_taps, space_taps, coregion_factor)
    out = out.reshape(2, DAYS, TILES, SLOTS, 128).transpose(0, 1, 3, 2, 4)
    return out.reshape(shape)


def solution(mesh):
    in_specs = (P(None, "day", "blk", None), P("blk"), P("blk", None), P(), P(), P())
    out_specs = P(None, "day", "blk", None)
    return jax.shard_map(shards, mesh=mesh, in_specs=in_specs, out_specs=out_specs, check_vma=False)
```

```python
import functools

import jax
import jax.numpy as jnp
from jax import lax
from jax.experimental import pallas as pl
from jax.experimental.pallas import tpu as pltpu
from jax.sharding import PartitionSpec as P

MESH = pl.DeviceIdType.MESH
REACH = 4
SLOTS = 8
DAYS = 3
SERIES = 2 * DAYS
TILES = 32
ROWS = TILES * SLOTS
STEP = 4
CHUNKS = (TILES - 4) // STEP
AHEAD = 0
EARLY = 4
EARLY_GROUPS = ((0, 1), (2, 3))
NONE = -(1 << 20)

EAST, WEST, NORTH, SOUTH, NE, NW, SE, SW = range(8)
PLACES = ((1, 0), (-1, 0), (1, -1), (-1, -1), (1, 1), (-1, 1))
OPPOSITE = (1, 0, 5, 4, 3, 2)


def kernel(
    x_hbm, nbr_hbm, act_hbm, time_hbm, space_hbm, factor_hbm, done,
    own, left, right, pack, pack_left, pack_right, pack_mixed, packs,
    mixed, strip_n, strip_s, halo, lhs, weights, side_lhs, side_weights, fix, across, swapped,
    take_index, take_mask, edge_mask, fix_mask, live_mask,
    nbr, act, time_taps, space_taps, factor,
    load_sem, small_sem, y_send, y_recv, z_send, z_recv, p_send, p_recv,
    days_ready, edges_ready,
):
    f32, bf16 = jnp.float32, jnp.bfloat16
    blk, day = lax.axis_index("blk"), lax.axis_index("day")
    blks, days = lax.axis_size("blk"), lax.axis_size("day")
    col, row, rows = blk % REACH, blk // REACH, blks // REACH

    has_left, has_right = day > 0, day < days - 1
    has_north, has_south = row > 0, row < rows - 1

    def place_exists(dx, dz):
        ok = (col + dx >= 0) & (col + dx < REACH)
        if dz:
            ok = ok & (row + dz >= 0) & (row + dz < rows)
        return ok

    small = [
        pltpu.make_async_copy(source, target, small_sem.at[index])
        for index, (source, target) in enumerate((
            (nbr_hbm, nbr), (act_hbm, act), (time_hbm, time_taps), (space_hbm, space_taps),
            (factor_hbm, factor),
        ))
    ]
    load = pltpu.make_async_copy(x_hbm, own, load_sem)
    load.start()
    for copy in small:
        copy.start()

    core = day % 2
    chip = day - core
    first_core, second_core = core == 0, core == 1
    barrier = pltpu.get_barrier_semaphore()

    def hello(there, db, to_day):
        @pl.when(there)
        def _():
            pl.semaphore_signal(
                barrier, inc=1, device_id={"blk": blk + db, "day": to_day}, device_id_type=MESH
            )

    def tell(sem, to_day):
        pl.semaphore_signal(
            sem, inc=1, device_id={"blk": blk, "day": to_day}, device_id_type=MESH
        )

    first_chip = day < 2
    hello(first_core & ~first_chip, 0, day + 1)
    hello(first_core & has_left, 0, day - 1)
    hello(second_core & has_right, 0, day + 2)
    hello(second_core & first_chip, 0, day - 1)
    expected_days = has_right.astype(jnp.int32) + 2 * (day > 1).astype(jnp.int32)
    expected_edges = first_chip.astype(jnp.int32)
    for there, db in [(has_north, -REACH), (has_south, REACH)] + [
        (place_exists(dx, dz), dx + REACH * dz) for dx, dz in PLACES
    ]:
        hello(there, db, chip)
        expected_edges = expected_edges + 2 * there.astype(jnp.int32)

    @pl.when(second_core)
    def _():
        pl.semaphore_wait(barrier, expected_days)

    @pl.when(second_core & ~first_chip)
    def _():
        tell(days_ready, day - 1)

    @pl.when(first_core & ~first_chip)
    def _():
        pl.semaphore_wait(days_ready, 1)

    def edges_entered():
        pl.semaphore_wait(barrier, expected_edges)
        tell(edges_ready, day + 1)

    @pl.when(first_core & first_chip)
    def _():
        edges_entered()

    def bulk_row(j):
        at = 16 + j * (STEP * SLOTS)
        return at if isinstance(j, int) else pl.multiple_of(at, 8)

    def y_copy(side, item):
        target = left if side == 0 else right
        if isinstance(item, int) and item == 0:
            source, target = pack, (pack_left if side == 0 else pack_right)
        else:
            if isinstance(item, int) and item < 3:
                span = pl.ds(0 if item == 1 else ROWS - 16, 16)
            else:
                span = pl.ds(bulk_row(item - 3), STEP * SLOTS)
            source, target = x_hbm.at[:, span, :], target.at[:, span, :]
        return pltpu.make_async_remote_copy(
            src_ref=source, dst_ref=target,
            send_sem=y_send.at[side, item], recv_sem=y_recv.at[side, item],
            device_id={"blk": blk, "day": day + (1 if side == 0 else -1)}, device_id_type=MESH,
        )

    for side, there in ((0, has_right), (1, day > 1)):
        @pl.when(there)
        def _(side=side):
            for item in range(1, 3 + AHEAD):
                y_copy(side, item).start()

    for copy in small:
        copy.wait()

    lane = lax.broadcasted_iota(jnp.int32, (SLOTS, 128), 1)
    cell = lane & 63
    low, high = cell < 4, cell >= 60
    slot = lax.broadcasted_iota(jnp.int32, (SLOTS, 128), 0)

    def named(direction):
        column = jnp.broadcast_to(nbr[:, direction : direction + 1], (SLOTS, 128))
        return jnp.where(column < 0, NONE, column)

    def on(target, db):
        first = (blk + db) * SLOTS
        return (target >= first) & (target < first + SLOTS)

    def sides(east, west):
        return jnp.where(low, named(east), jnp.where(high, named(west), NONE))

    for index, (target, db) in enumerate((
        (sides(EAST, WEST), 0),
        (named(NORTH), -REACH), (sides(NE, NW), -REACH),
        (named(SOUTH), REACH), (sides(SE, SW), REACH),
    )):
        take_index[index] = target & (SLOTS - 1)
        take_mask[index] = jnp.where(on(target, db), 1.0, 0.0).astype(f32)
    for index, (east, west, dz) in enumerate(((EAST, WEST, 0), (NE, NW, -1), (SE, SW, 1))):
        there = (low & on(named(east), REACH * dz + 1)) | (high & on(named(west), REACH * dz - 1))
        edge_mask[index] = jnp.where(there, 1.0, 0.0).astype(f32)
    there = (high & on(named(EAST), 1)) | (low & on(named(WEST), -1))
    fix_mask[...] = jnp.where(there, 1.0, 0.0).astype(f32)
    at_east = on(named(EAST), 1) | on(named(NE), 1 - REACH) | on(named(SE), 1 + REACH)
    at_west = on(named(WEST), -1) | on(named(NW), -1 - REACH) | on(named(SW), -1 + REACH)
    ends = jnp.where((high & at_east) | (low & at_west), 1.0, 0.0).astype(f32)
    end_slot = jnp.broadcast_to(
        jnp.sum(ends * slot.astype(f32), axis=0, keepdims=True), (SLOTS, 128)
    ).astype(jnp.int32)
    end_mask = jnp.broadcast_to(jnp.sum(ends, axis=0, keepdims=True), (SLOTS, 128))
    live = jnp.zeros((SLOTS, 128), f32)
    for s in range(SLOTS):
        live = jnp.where(slot == s, act[s].astype(f32), live)
    live_mask[...] = live

    @pl.when(jnp.logical_not(has_left))
    def _():
        pack_left[...] = jnp.zeros_like(pack_left)

        def clear(i, carry):
            left[i] = jnp.zeros((ROWS, 128), f32)
            return carry

        lax.fori_loop(0, SERIES, clear, 0)

    @pl.when(jnp.logical_not(has_right))
    def _():
        pack_right[...] = jnp.zeros_like(pack_right)

        def clear(i, carry):
            right[i] = jnp.zeros((ROWS, 128), f32)
            return carry

        lax.fori_loop(0, SERIES, clear, 0)

    @pl.when(jnp.logical_not(has_north))
    def _():
        strip_n[...] = jnp.zeros_like(strip_n)

    @pl.when(jnp.logical_not(has_south))
    def _():
        strip_s[...] = jnp.zeros_like(strip_s)

    for index, (dx, dz) in enumerate(PLACES):
        @pl.when(jnp.logical_not(place_exists(dx, dz)))
        def _(index=index):
            packs[index] = jnp.zeros((DAYS * SLOTS, 128), f32)

    load.wait()

    for t in range(DAYS):
        total = jnp.zeros((SLOTS, 128), f32)
        for c in range(2):
            for q in range(4):
                part = None
                for g in range(SLOTS):
                    value = own[c * DAYS + t, pl.ds((4 * g + q) * SLOTS, SLOTS), :]
                    value = jnp.take_along_axis(value, end_slot, axis=0)
                    part = value if part is None else jnp.where(slot == g, value, part)
                part = part * end_mask
                shift = 8 * (4 * c + q)
                total = total + (pltpu.roll(part, shift, 1) if shift else part)
        pack[t * SLOTS : (t + 1) * SLOTS, :] = total

    def send_rest(side):
        y_copy(side, 0).start()

        def send(j, carry):
            y_copy(side, j).start()
            return carry

        lax.fori_loop(3 + AHEAD, 3 + CHUNKS, send, 0)

    for side, there in ((0, has_right), (1, day > 1)):
        @pl.when(there)
        def _(side=side):
            send_rest(side)

    @pl.when(second_core & first_chip)
    def _():
        pl.semaphore_wait(edges_ready, 1)
        for item in range(1, 3 + AHEAD):
            y_copy(1, item).start()
        send_rest(1)

    def y_wait(item):
        for side, there in ((0, has_left), (1, has_right)):
            @pl.when(there)
            def _(side=side):
                y_copy(side, item).wait_recv()

    w = [time_taps[k] for k in range(DAYS + 1)]
    a = [space_taps[0, k] for k in range(5)]
    d = [space_taps[1, k] for k in range(5)]
    k00 = factor[0, 0] * factor[0, 0] + factor[0, 1] * factor[0, 1]
    k01 = factor[0, 0] * factor[1, 0] + factor[0, 1] * factor[1, 1]
    k11 = factor[1, 0] * factor[1, 0] + factor[1, 1] * factor[1, 1]

    k = lax.broadcasted_iota(jnp.int32, (256, 256), 0)
    n = lax.broadcasted_iota(jnp.int32, (256, 256), 1)
    place = k & 63
    beyond = jnp.where(place < 4, place + 64, jnp.where(place >= 60, place - 64, 1024))
    place = jnp.where(k >= 128, beyond, place)
    distance = jnp.abs(place - (n & 63))
    same_row = ((k >> 6) & 1) == (((n >> 6) ^ (n >> 7)) & 1)
    weight = jnp.zeros((256, 256), f32)
    for tap in range(5):
        weight = jnp.where(same_row & (distance == tap), a[tap], weight)
    weight_high = weight.astype(bf16)
    weights[0:256, :] = weight_high
    weights[256:512, :] = weight_high
    weight_low = (weight - weight_high.astype(f32)).astype(bf16)
    weights[512:768, :] = weight_low
    side_weights[0:128, :] = weight_high[128:]
    side_weights[128:256, :] = weight_high[128:]
    side_weights[256:384, :] = weight_low[128:]

    def filtered(v):
        return [
            w[0] * v[t + 3] + w[1] * (v[t + 2] + v[t + 4])
            + w[2] * (v[t + 1] + v[t + 5]) + w[3] * (v[t] + v[t + 6])
            for t in range(DAYS)
        ]

    def mix_tile(at):
        span = pl.ds(at, SLOTS)
        f = []
        for c in range(2):
            v = [ref[c * DAYS + t, span, :] for ref in (left, own, right) for t in range(DAYS)]
            f.append(filtered(v))
        m = live_mask[...]
        for t in range(DAYS):
            mixed[t, span, :] = (k00 * f[0][t] + k01 * f[1][t]) * m
            mixed[DAYS + t, span, :] = (k01 * f[0][t] + k11 * f[1][t]) * m

    def p_copy(index):
        dx, dz = PLACES[index]
        return pltpu.make_async_remote_copy(
            src_ref=pack_mixed, dst_ref=packs.at[OPPOSITE[index]],
            send_sem=p_send.at[index], recv_sem=p_recv.at[OPPOSITE[index]],
            device_id={"blk": blk + dx + REACH * dz, "day": day}, device_id_type=MESH,
        )

    def p_arrival(index):
        return pltpu.make_async_remote_copy(
            src_ref=pack_mixed, dst_ref=packs.at[index],
            send_sem=p_send.at[index], recv_sem=p_recv.at[index],
            device_id={"blk": blk, "day": day}, device_id_type=MESH,
        )

    def z_copy(side):
        span = pl.ds(ROWS - 16, 16) if side == 0 else pl.ds(0, 16)
        return pltpu.make_async_remote_copy(
            src_ref=mixed.at[:, span, :], dst_ref=strip_n if side == 0 else strip_s,
            send_sem=z_send.at[side], recv_sem=z_recv.at[side],
            device_id={"blk": blk + (REACH if side == 0 else -REACH), "day": day},
            device_id_type=MESH,
        )

    y_wait(0)
    v = [
        ref[t * SLOTS : (t + 1) * SLOTS, :]
        for ref in (pack_left, pack, pack_right) for t in range(DAYS)
    ]
    second = (((lane + 68) >> 3) & 7) >= 4
    for t, f in enumerate(filtered(v)):
        first_part = k00 * f + k01 * pltpu.roll(f, 96, 1)
        second_part = k11 * f + k01 * pltpu.roll(f, 32, 1)
        pack_mixed[t * SLOTS : (t + 1) * SLOTS, :] = jnp.where(second, second_part, first_part)

    @pl.when(first_core & ~first_chip)
    def _():
        edges_entered()

    @pl.when(second_core & ~first_chip)
    def _():
        pl.semaphore_wait(edges_ready, 1)

    for index, (dx, dz) in enumerate(PLACES):
        @pl.when(place_exists(dx, dz))
        def _(index=index):
            p_copy(index).start()

    for item in (1, 2):
        y_wait(item)
    for tile in (0, 1, TILES - 2, TILES - 1):
        mix_tile(tile * SLOTS)

    for side, there in ((0, has_south), (1, has_north)):
        @pl.when(there)
        def _(side=side):
            z_copy(side).start()

    def take(value, index):
        return jnp.take_along_axis(value, take_index[index], axis=0) * take_mask[index]

    def own_side(series, at):
        return take(mixed[series, pl.ds(at, SLOTS), :], 0)

    def split(value):
        top = value.astype(bf16)
        return top, (value - top.astype(f32)).astype(bf16)

    block_rows = SERIES * STEP * SLOTS

    def stage(series, centres, side_tiles, block=0):
        at = block * block_rows + series * (STEP * SLOTS)
        span = pl.ds(pl.multiple_of(at, 8), STEP * SLOTS)
        for column, value in ((0, centres), (128, jnp.concatenate(side_tiles, axis=0))):
            top, rest = split(value)
            lhs[span, column : column + 128] = top
            lhs[span, 256 + column : 384 + column] = rest

    def filter_across(*blocks):
        count = len(blocks) * block_rows
        result = jnp.dot(lhs[0:count, :], weights[0:512, :], preferred_element_type=f32)
        result = result + jnp.dot(
            lhs[0:count, 0:256], weights[512:768, :], preferred_element_type=f32
        )
        half = STEP * SLOTS // 2
        for block, places in enumerate(blocks):
            for series in range(SERIES):
                for n, at in enumerate(places):
                    row = block * block_rows + (2 * series + n) * half
                    part = result[row : row + half]
                    across[series, pl.ds(at, half), :] = part[:, :128]
                    swapped[series, pl.ds(at, half), :] = part[:, 128:]

    def stage_chunk(j, sides_of, block=0):
        first = bulk_row(j)

        def stage_step(series, inner):
            side_tiles = [sides_of(series, first + n * SLOTS, n) for n in range(STEP)]
            centres = mixed[series, pl.ds(first, STEP * SLOTS), :]
            stage(series, centres, side_tiles, block)
            return inner

        lax.fori_loop(0, SERIES, stage_step, 0)
        return first + 16, first + 32

    def rim_stage(series, carry):
        spots = [tile * SLOTS for tile in (0, 1, TILES - 2, TILES - 1)]
        centres = [mixed[series, at : at + SLOTS, :] for at in spots]
        stage(series, jnp.concatenate(centres, axis=0), [own_side(series, at) for at in spots])
        return carry

    lax.fori_loop(0, SERIES, rim_stage, 0)
    blocks = [(16, ROWS)]

    def mix_chunk(j, carry):
        y_wait(j + 3)
        for n in range(STEP):
            mix_tile(bulk_row(j) + n * SLOTS)
        return carry

    for group in EARLY_GROUPS:
        lax.fori_loop(group[0], group[-1] + 1, mix_chunk, 0)
        for j in group:
            blocks.append(stage_chunk(j, lambda series, at, n: own_side(series, at), len(blocks)))
        filter_across(*blocks)
        blocks = []

    for index, (dx, dz) in enumerate(PLACES):
        @pl.when(place_exists(dx, dz))
        def _(index=index):
            p_arrival(index).wait_recv()

    west_lanes = (lane & 7) < 4
    for t in range(DAYS):
        span = slice(t * SLOTS, (t + 1) * SLOTS)
        for index in range(3):
            both = jnp.where(west_lanes, packs[2 * index, span, :], packs[2 * index + 1, span, :])
            for c in range(2):
                for q in range(4):
                    shift = 8 * (4 * c + q)
                    value = pltpu.roll(both, 128 - shift, 1) if shift else both
                    halo[index, c * DAYS + t, q] = value

    def side_stage(series, carry):
        span = pl.ds(pl.multiple_of(series * (4 * SLOTS), 8), 4 * SLOTS)
        value = jnp.concatenate([halo[0, series, q] for q in range(4)], axis=0)
        top, rest = split(value)
        side_lhs[span, 0:128] = top
        side_lhs[span, 128:256] = rest
        side_lhs[span, 256:384] = top
        return carry

    lax.fori_loop(0, SERIES, side_stage, 0)
    added = jnp.dot(side_lhs[...], side_weights[...], preferred_element_type=f32)
    fix[0] = added[:, :128]
    fix[1] = added[:, 128:]

    for side, there in ((0, has_north), (1, has_south)):
        @pl.when(there)
        def _(side=side):
            z_copy(side).wait_recv()

    def outer_stage(series, carry):
        centres, side_tiles = [], []
        for strip, index, edge, tiles, g in (
            (strip_n, 1, 1, (2, 3), SLOTS - 1), (strip_s, 3, 2, (0, 1), 0)
        ):
            for n, q in enumerate(tiles):
                value = strip[series, n * SLOTS : (n + 1) * SLOTS, :]
                centres.append(take(value, index))
                side = halo[edge, series, q, g : g + 1, :] * edge_mask[edge]
                side_tiles.append(take(value, index + 1) + side)
        stage(series, jnp.concatenate(centres, axis=0), side_tiles)
        return carry

    lax.fori_loop(0, SERIES, outer_stage, 0)
    filter_across((0, ROWS + 16))

    def add_fix(series, at, g, q):
        row = (series * 4 + q) * SLOTS + g
        span = pl.ds(at + 2 * SLOTS, SLOTS)
        m = fix_mask[...]
        across[series, span, :] = across[series, span, :] + fix[0, pl.ds(row, 1), :] * m
        swapped[series, span, :] = swapped[series, span, :] + fix[1, pl.ds(row, 1), :] * m

    def rim_fix(series, carry):
        for tile in (0, 1, TILES - 2, TILES - 1):
            add_fix(series, tile * SLOTS, tile // 4, tile % 4)
        return carry

    lax.fori_loop(0, SERIES, rim_fix, 0)

    first_half = lane < 64

    def filter_down(series, tile):
        base = tile * SLOTS
        m = live_mask[...]
        s = [across[series, pl.ds(base + SLOTS * n, SLOTS), :] for n in range(STEP + 4)]
        b = [swapped[series, pl.ds(base + SLOTS * n, SLOTS), :] for n in range(STEP + 4)]
        o = [jnp.where(first_half, b[n], b[n + 1]) for n in range(STEP + 3)]
        for n in range(STEP):
            total = (
                d[0] * s[n + 2] + d[1] * (o[n + 2] + o[n + 1]) + d[2] * (s[n + 3] + s[n + 1])
                + d[3] * (o[n + 3] + o[n]) + d[4] * (s[n + 4] + s[n])
            )
            done[series, pl.ds(base + SLOTS * n, SLOTS), :] = total * m

    def late_down(j, carry):
        def down_step(series, inner):
            filter_down(series, j * STEP)
            return inner

        return lax.fori_loop(0, SERIES, down_step, carry)

    def fixed_down(j, carry):
        first = bulk_row(j)

        def down_step(series, inner):
            for n in range(STEP):
                add_fix(series, first + n * SLOTS, j + (2 + n) // 4, (2 + n) % 4)
            filter_down(series, j * STEP)
            return inner

        return lax.fori_loop(0, SERIES, down_step, carry)

    lax.fori_loop(0, EARLY, fixed_down, 0)

    def bulk(j, carry):
        mix_chunk(j, carry)

        def sides_of(series, at, n):
            row = halo[0, series, (2 + n) % 4, pl.ds(j + (2 + n) // 4, 1), :]
            return own_side(series, at) + row * edge_mask[0]

        filter_across(stage_chunk(j, sides_of))
        return late_down(j, carry)

    lax.fori_loop(EARLY, CHUNKS, bulk, 0)

    def last_step(series, carry):
        filter_down(series, TILES - STEP)
        return carry

    lax.fori_loop(0, SERIES, last_step, 0)

    for side, there in ((0, has_right), (1, has_left)):
        @pl.when(there)
        def _(side=side):
            for item in range(3):
                y_copy(side, item).wait_send()

            def sent(j, carry):
                y_copy(side, j).wait_send()
                return carry

            lax.fori_loop(3, 3 + CHUNKS, sent, 0)

    for index, (dx, dz) in enumerate(PLACES):
        @pl.when(place_exists(dx, dz))
        def _(index=index):
            p_copy(index).wait_send()

    for side, there in ((0, has_south), (1, has_north)):
        @pl.when(there)
        def _(side=side):
            z_copy(side).wait_send()


def shards(input_field, active_mask, neighbours, time_taps, space_taps, coregion_factor):
    shape = input_field.shape
    tiles = input_field.reshape(2, DAYS, SLOTS, TILES, 128).transpose(0, 1, 3, 2, 4)
    tiles = tiles.reshape(SERIES, ROWS, 128)
    f32 = jnp.float32
    vmem = pltpu.VMEM
    dma = pltpu.SemaphoreType.DMA
    out = pl.pallas_call(
        kernel,
        out_shape=vmem((SERIES, ROWS, 128), f32),
        in_specs=[pl.BlockSpec(memory_space=pl.ANY)] * 6,
        out_specs=pl.BlockSpec(memory_space=vmem),
        scratch_shapes=[
            vmem((SERIES, ROWS, 128), f32),
            vmem((SERIES, ROWS, 128), f32),
            vmem((SERIES, ROWS, 128), f32),
            vmem((DAYS * SLOTS, 128), f32),
            vmem((DAYS * SLOTS, 128), f32),
            vmem((DAYS * SLOTS, 128), f32),
            vmem((DAYS * SLOTS, 128), f32),
            vmem((6, DAYS * SLOTS, 128), f32),
            vmem((SERIES, ROWS, 128), f32),
            vmem((SERIES, 16, 128), f32),
            vmem((SERIES, 16, 128), f32),
            vmem((3, SERIES, 4, SLOTS, 128), f32),
            vmem((3 * SERIES * STEP * SLOTS, 512), jnp.bfloat16),
            vmem((768, 256), jnp.bfloat16),
            vmem((SERIES * 4 * SLOTS, 384), jnp.bfloat16),
            vmem((384, 256), jnp.bfloat16),
            vmem((2, SERIES * 4 * SLOTS, 128), f32),
            vmem((SERIES, ROWS + 32, 128), f32),
            vmem((SERIES, ROWS + 32, 128), f32),
            vmem((5, SLOTS, 128), jnp.int32),
            vmem((5, SLOTS, 128), f32),
            vmem((3, SLOTS, 128), f32),
            vmem((SLOTS, 128), f32),
            vmem((SLOTS, 128), f32),
            vmem((SLOTS, 8), jnp.int32),
            pltpu.SMEM((SLOTS,), jnp.int32),
            pltpu.SMEM((DAYS + 1,), f32),
            pltpu.SMEM((2, 5), f32),
            pltpu.SMEM((2, 2), f32),
            dma,
            dma((5,)),
            dma((2, 3 + CHUNKS)),
            dma((2, 3 + CHUNKS)),
            dma((2,)),
            dma((2,)),
            dma((6,)),
            dma((6,)),
            pltpu.SemaphoreType.REGULAR,
            pltpu.SemaphoreType.REGULAR,
        ],
        compiler_params=pltpu.CompilerParams(collective_id=0, has_side_effects=True),
    )(tiles, neighbours, active_mask, time_taps, space_taps, coregion_factor)
    out = out.reshape(2, DAYS, TILES, SLOTS, 128).transpose(0, 1, 3, 2, 4)
    return out.reshape(shape)


def solution(mesh):
    in_specs = (P(None, "day", "blk", None), P("blk"), P("blk", None), P(), P(), P())
    out_specs = P(None, "day", "blk", None)
    return jax.shard_map(shards, mesh=mesh, in_specs=in_specs, out_specs=out_specs, check_vma=False)
```

```python
import functools

import jax
import jax.numpy as jnp
from jax import lax
from jax.experimental import pallas as pl
from jax.experimental.pallas import tpu as pltpu
from jax.sharding import PartitionSpec as P

MESH = pl.DeviceIdType.MESH
REACH = 4
SLOTS = 8
DAYS = 3
SERIES = 2 * DAYS
TILES = 32
ROWS = TILES * SLOTS
STEP = 4
CHUNKS = (TILES - 4) // STEP
AHEAD = 0
EARLY = 4
LAST = 8
EARLY_GROUPS = ((0, 1), (2, 3))
NONE = -(1 << 20)

EAST, WEST, NORTH, SOUTH, NE, NW, SE, SW = range(8)
PLACES = ((1, 0), (-1, 0), (1, -1), (-1, -1), (1, 1), (-1, 1))
OPPOSITE = (1, 0, 5, 4, 3, 2)


def kernel(
    x_hbm, nbr_hbm, act_hbm, time_hbm, space_hbm, factor_hbm, done, across, swapped, shared,
    own, left, right, pack, pack_left, pack_right, pack_mixed, packs,
    mixed, strip_n, strip_s, halo, lhs, weights, side_lhs, side_weights, fix,
    take_index, take_mask, edge_mask, fix_mask, live_mask,
    nbr, act, time_taps, space_taps, factor,
    load_sem, small_sem, y_send, y_recv, z_send, z_recv, p_send, p_recv,
    days_ready, edges_ready,
):
    f32, bf16 = jnp.float32, jnp.bfloat16
    blk, day = lax.axis_index("blk"), lax.axis_index("day")
    blks, days = lax.axis_size("blk"), lax.axis_size("day")
    col, row, rows = blk % REACH, blk // REACH, blks // REACH

    has_left, has_right = day > 0, day < days - 1
    has_north, has_south = row > 0, row < rows - 1

    def place_exists(dx, dz):
        ok = (col + dx >= 0) & (col + dx < REACH)
        if dz:
            ok = ok & (row + dz >= 0) & (row + dz < rows)
        return ok

    small = [
        pltpu.make_async_copy(source, target, small_sem.at[index])
        for index, (source, target) in enumerate((
            (nbr_hbm, nbr), (act_hbm, act), (time_hbm, time_taps), (space_hbm, space_taps),
            (factor_hbm, factor),
        ))
    ]
    load = pltpu.make_async_copy(x_hbm, own, load_sem)
    load.start()
    for copy in small:
        copy.start()

    core = day % 2
    chip = day - core
    first_core, second_core = core == 0, core == 1
    barrier = pltpu.get_barrier_semaphore()

    def hello(there, db, to_day):
        @pl.when(there)
        def _():
            pl.semaphore_signal(
                barrier, inc=1, device_id={"blk": blk + db, "day": to_day}, device_id_type=MESH
            )

    def tell(sem, to_day):
        pl.semaphore_signal(
            sem, inc=1, device_id={"blk": blk, "day": to_day}, device_id_type=MESH
        )

    first_chip = day < 2
    hello(first_core & ~first_chip, 0, day + 1)
    hello(first_core & has_left, 0, day - 1)
    hello(second_core & has_right, 0, day + 2)
    hello(second_core & first_chip, 0, day - 1)
    expected_days = has_right.astype(jnp.int32) + 2 * (day > 1).astype(jnp.int32)
    expected_edges = first_chip.astype(jnp.int32)
    for there, db in [(has_north, -REACH), (has_south, REACH)] + [
        (place_exists(dx, dz), dx + REACH * dz) for dx, dz in PLACES
    ]:
        hello(there, db, chip)
        expected_edges = expected_edges + 2 * there.astype(jnp.int32)

    @pl.when(second_core)
    def _():
        pl.semaphore_wait(barrier, expected_days)

    @pl.when(second_core & ~first_chip)
    def _():
        tell(days_ready, day - 1)

    @pl.when(first_core & ~first_chip)
    def _():
        pl.semaphore_wait(days_ready, 1)

    def edges_entered():
        pl.semaphore_wait(barrier, expected_edges)
        tell(edges_ready, day + 1)

    @pl.when(first_core & first_chip)
    def _():
        edges_entered()

    def bulk_row(j):
        at = 16 + j * (STEP * SLOTS)
        return at if isinstance(j, int) else pl.multiple_of(at, 8)

    def y_copy(side, item):
        target = left if side == 0 else right
        if isinstance(item, int) and item == 0:
            source, target = pack, (pack_left if side == 0 else pack_right)
        else:
            if isinstance(item, int) and item < 3:
                span = pl.ds(0 if item == 1 else ROWS - 16, 16)
            else:
                span = pl.ds(bulk_row(item - 3), STEP * SLOTS)
            source, target = x_hbm.at[:, span, :], target.at[:, span, :]
        return pltpu.make_async_remote_copy(
            src_ref=source, dst_ref=target,
            send_sem=y_send.at[side, item], recv_sem=y_recv.at[side, item],
            device_id={"blk": blk, "day": day + (1 if side == 0 else -1)}, device_id_type=MESH,
        )

    for side, there in ((0, has_right), (1, day > 1)):
        @pl.when(there)
        def _(side=side):
            for item in range(1, 3 + AHEAD):
                y_copy(side, item).start()

    for copy in small:
        copy.wait()

    lane = lax.broadcasted_iota(jnp.int32, (SLOTS, 128), 1)
    cell = lane & 63
    low, high = cell < 4, cell >= 60
    slot = lax.broadcasted_iota(jnp.int32, (SLOTS, 128), 0)

    def named(direction):
        column = jnp.broadcast_to(nbr[:, direction : direction + 1], (SLOTS, 128))
        return jnp.where(column < 0, NONE, column)

    def on(target, db):
        first = (blk + db) * SLOTS
        return (target >= first) & (target < first + SLOTS)

    def sides(east, west):
        return jnp.where(low, named(east), jnp.where(high, named(west), NONE))

    for index, (target, db) in enumerate((
        (sides(EAST, WEST), 0),
        (named(NORTH), -REACH), (sides(NE, NW), -REACH),
        (named(SOUTH), REACH), (sides(SE, SW), REACH),
    )):
        take_index[index] = target & (SLOTS - 1)
        take_mask[index] = jnp.where(on(target, db), 1.0, 0.0).astype(f32)
    for index, (east, west, dz) in enumerate(((EAST, WEST, 0), (NE, NW, -1), (SE, SW, 1))):
        there = (low & on(named(east), REACH * dz + 1)) | (high & on(named(west), REACH * dz - 1))
        edge_mask[index] = jnp.where(there, 1.0, 0.0).astype(f32)
    there = (high & on(named(EAST), 1)) | (low & on(named(WEST), -1))
    fix_mask[...] = jnp.where(there, 1.0, 0.0).astype(f32)
    at_east = on(named(EAST), 1) | on(named(NE), 1 - REACH) | on(named(SE), 1 + REACH)
    at_west = on(named(WEST), -1) | on(named(NW), -1 - REACH) | on(named(SW), -1 + REACH)
    ends = jnp.where((high & at_east) | (low & at_west), 1.0, 0.0).astype(f32)
    end_slot = jnp.broadcast_to(
        jnp.sum(ends * slot.astype(f32), axis=0, keepdims=True), (SLOTS, 128)
    ).astype(jnp.int32)
    end_mask = jnp.broadcast_to(jnp.sum(ends, axis=0, keepdims=True), (SLOTS, 128))
    live = jnp.zeros((SLOTS, 128), f32)
    for s in range(SLOTS):
        live = jnp.where(slot == s, act[s].astype(f32), live)
    live_mask[...] = live
    shared[0:SLOTS, :] = live
    for tap in range(5):
        shared[SLOTS + tap : SLOTS + tap + 1, :] = jnp.full((1, 128), space_taps[1, tap], f32)

    @pl.when(jnp.logical_not(has_left))
    def _():
        pack_left[...] = jnp.zeros_like(pack_left)

        def clear(i, carry):
            left[i] = jnp.zeros((ROWS, 128), f32)
            return carry

        lax.fori_loop(0, SERIES, clear, 0)

    @pl.when(jnp.logical_not(has_right))
    def _():
        pack_right[...] = jnp.zeros_like(pack_right)

        def clear(i, carry):
            right[i] = jnp.zeros((ROWS, 128), f32)
            return carry

        lax.fori_loop(0, SERIES, clear, 0)

    @pl.when(jnp.logical_not(has_north))
    def _():
        strip_n[...] = jnp.zeros_like(strip_n)

    @pl.when(jnp.logical_not(has_south))
    def _():
        strip_s[...] = jnp.zeros_like(strip_s)

    for index, (dx, dz) in enumerate(PLACES):
        @pl.when(jnp.logical_not(place_exists(dx, dz)))
        def _(index=index):
            packs[index] = jnp.zeros((DAYS * SLOTS, 128), f32)

    load.wait()

    for t in range(DAYS):
        total = jnp.zeros((SLOTS, 128), f32)
        for c in range(2):
            for q in range(4):
                part = None
                for g in range(SLOTS):
                    value = own[c * DAYS + t, pl.ds((4 * g + q) * SLOTS, SLOTS), :]
                    value = jnp.take_along_axis(value, end_slot, axis=0)
                    part = value if part is None else jnp.where(slot == g, value, part)
                part = part * end_mask
                shift = 8 * (4 * c + q)
                total = total + (pltpu.roll(part, shift, 1) if shift else part)
        pack[t * SLOTS : (t + 1) * SLOTS, :] = total

    def send_rest(side):
        y_copy(side, 0).start()

        def send(j, carry):
            y_copy(side, j).start()
            return carry

        lax.fori_loop(3 + AHEAD, 3 + CHUNKS, send, 0)

    for side, there in ((0, has_right), (1, day > 1)):
        @pl.when(there)
        def _(side=side):
            send_rest(side)

    @pl.when(second_core & first_chip)
    def _():
        pl.semaphore_wait(edges_ready, 1)
        for item in range(1, 3 + AHEAD):
            y_copy(1, item).start()
        send_rest(1)

    def y_wait(item):
        for side, there in ((0, has_left), (1, has_right)):
            @pl.when(there)
            def _(side=side):
                y_copy(side, item).wait_recv()

    w = [time_taps[k] for k in range(DAYS + 1)]
    a = [space_taps[0, k] for k in range(5)]
    d = [space_taps[1, k] for k in range(5)]
    k00 = factor[0, 0] * factor[0, 0] + factor[0, 1] * factor[0, 1]
    k01 = factor[0, 0] * factor[1, 0] + factor[0, 1] * factor[1, 1]
    k11 = factor[1, 0] * factor[1, 0] + factor[1, 1] * factor[1, 1]

    k = lax.broadcasted_iota(jnp.int32, (256, 256), 0)
    n = lax.broadcasted_iota(jnp.int32, (256, 256), 1)
    place = k & 63
    beyond = jnp.where(place < 4, place + 64, jnp.where(place >= 60, place - 64, 1024))
    place = jnp.where(k >= 128, beyond, place)
    distance = jnp.abs(place - (n & 63))
    same_row = ((k >> 6) & 1) == (((n >> 6) ^ (n >> 7)) & 1)
    weight = jnp.zeros((256, 256), f32)
    for tap in range(5):
        weight = jnp.where(same_row & (distance == tap), a[tap], weight)
    weight_high = weight.astype(bf16)
    weights[0:256, :] = weight_high
    weights[256:512, :] = weight_high
    weight_low = (weight - weight_high.astype(f32)).astype(bf16)
    weights[512:768, :] = weight_low
    side_weights[0:128, :] = weight_high[128:]
    side_weights[128:256, :] = weight_high[128:]
    side_weights[256:384, :] = weight_low[128:]

    def filtered(v):
        return [
            w[0] * v[t + 3] + w[1] * (v[t + 2] + v[t + 4])
            + w[2] * (v[t + 1] + v[t + 5]) + w[3] * (v[t] + v[t + 6])
            for t in range(DAYS)
        ]

    def mix_tile(at):
        span = pl.ds(at, SLOTS)
        f = []
        for c in range(2):
            v = [ref[c * DAYS + t, span, :] for ref in (left, own, right) for t in range(DAYS)]
            f.append(filtered(v))
        m = live_mask[...]
        for t in range(DAYS):
            mixed[t, span, :] = (k00 * f[0][t] + k01 * f[1][t]) * m
            mixed[DAYS + t, span, :] = (k01 * f[0][t] + k11 * f[1][t]) * m

    def p_copy(index):
        dx, dz = PLACES[index]
        return pltpu.make_async_remote_copy(
            src_ref=pack_mixed, dst_ref=packs.at[OPPOSITE[index]],
            send_sem=p_send.at[index], recv_sem=p_recv.at[OPPOSITE[index]],
            device_id={"blk": blk + dx + REACH * dz, "day": day}, device_id_type=MESH,
        )

    def p_arrival(index):
        return pltpu.make_async_remote_copy(
            src_ref=pack_mixed, dst_ref=packs.at[index],
            send_sem=p_send.at[index], recv_sem=p_recv.at[index],
            device_id={"blk": blk, "day": day}, device_id_type=MESH,
        )

    def z_copy(side):
        span = pl.ds(ROWS - 16, 16) if side == 0 else pl.ds(0, 16)
        return pltpu.make_async_remote_copy(
            src_ref=mixed.at[:, span, :], dst_ref=strip_n if side == 0 else strip_s,
            send_sem=z_send.at[side], recv_sem=z_recv.at[side],
            device_id={"blk": blk + (REACH if side == 0 else -REACH), "day": day},
            device_id_type=MESH,
        )

    y_wait(0)
    v = [
        ref[t * SLOTS : (t + 1) * SLOTS, :]
        for ref in (pack_left, pack, pack_right) for t in range(DAYS)
    ]
    second = (((lane + 68) >> 3) & 7) >= 4
    for t, f in enumerate(filtered(v)):
        first_part = k00 * f + k01 * pltpu.roll(f, 96, 1)
        second_part = k11 * f + k01 * pltpu.roll(f, 32, 1)
        pack_mixed[t * SLOTS : (t + 1) * SLOTS, :] = jnp.where(second, second_part, first_part)

    @pl.when(first_core & ~first_chip)
    def _():
        edges_entered()

    @pl.when(second_core & ~first_chip)
    def _():
        pl.semaphore_wait(edges_ready, 1)

    for index, (dx, dz) in enumerate(PLACES):
        @pl.when(place_exists(dx, dz))
        def _(index=index):
            p_copy(index).start()

    for item in (1, 2):
        y_wait(item)
    for tile in (0, 1, TILES - 2, TILES - 1):
        mix_tile(tile * SLOTS)

    for side, there in ((0, has_south), (1, has_north)):
        @pl.when(there)
        def _(side=side):
            z_copy(side).start()

    def take(value, index):
        return jnp.take_along_axis(value, take_index[index], axis=0) * take_mask[index]

    def own_side(series, at):
        return take(mixed[series, pl.ds(at, SLOTS), :], 0)

    def split(value):
        top = value.astype(bf16)
        return top, (value - top.astype(f32)).astype(bf16)

    block_rows = SERIES * STEP * SLOTS

    def stage(series, centres, side_tiles, block=0):
        at = block * block_rows + series * (STEP * SLOTS)
        span = pl.ds(pl.multiple_of(at, 8), STEP * SLOTS)
        for column, value in ((0, centres), (128, jnp.concatenate(side_tiles, axis=0))):
            top, rest = split(value)
            lhs[span, column : column + 128] = top
            lhs[span, 256 + column : 384 + column] = rest

    def filter_across(*blocks):
        count = len(blocks) * block_rows
        result = jnp.dot(lhs[0:count, :], weights[0:512, :], preferred_element_type=f32)
        result = result + jnp.dot(
            lhs[0:count, 0:256], weights[512:768, :], preferred_element_type=f32
        )
        half = STEP * SLOTS // 2
        for block, places in enumerate(blocks):
            for series in range(SERIES):
                for n, at in enumerate(places):
                    row = block * block_rows + (2 * series + n) * half
                    part = result[row : row + half]
                    across[series, pl.ds(at, half), :] = part[:, :128]
                    swapped[series, pl.ds(at, half), :] = part[:, 128:]

    def stage_chunk(j, sides_of, block=0):
        first = bulk_row(j)

        def stage_step(series, inner):
            side_tiles = [sides_of(series, first + n * SLOTS, n) for n in range(STEP)]
            centres = mixed[series, pl.ds(first, STEP * SLOTS), :]
            stage(series, centres, side_tiles, block)
            return inner

        lax.fori_loop(0, SERIES, stage_step, 0)
        return first + 16, first + 32

    def rim_stage(series, carry):
        spots = [tile * SLOTS for tile in (0, 1, TILES - 2, TILES - 1)]
        centres = [mixed[series, at : at + SLOTS, :] for at in spots]
        stage(series, jnp.concatenate(centres, axis=0), [own_side(series, at) for at in spots])
        return carry

    lax.fori_loop(0, SERIES, rim_stage, 0)
    blocks = [(16, ROWS)]

    def mix_chunk(j, carry):
        y_wait(j + 3)
        for n in range(STEP):
            mix_tile(bulk_row(j) + n * SLOTS)
        return carry

    for group in EARLY_GROUPS:
        lax.fori_loop(group[0], group[-1] + 1, mix_chunk, 0)
        for j in group:
            blocks.append(stage_chunk(j, lambda series, at, n: own_side(series, at), len(blocks)))
        filter_across(*blocks)
        blocks = []

    for index, (dx, dz) in enumerate(PLACES):
        @pl.when(place_exists(dx, dz))
        def _(index=index):
            p_arrival(index).wait_recv()

    west_lanes = (lane & 7) < 4
    for t in range(DAYS):
        span = slice(t * SLOTS, (t + 1) * SLOTS)
        for index in range(3):
            both = jnp.where(west_lanes, packs[2 * index, span, :], packs[2 * index + 1, span, :])
            for c in range(2):
                for q in range(4):
                    shift = 8 * (4 * c + q)
                    value = pltpu.roll(both, 128 - shift, 1) if shift else both
                    halo[index, c * DAYS + t, q] = value

    def side_stage(series, carry):
        span = pl.ds(pl.multiple_of(series * (4 * SLOTS), 8), 4 * SLOTS)
        value = jnp.concatenate([halo[0, series, q] for q in range(4)], axis=0)
        top, rest = split(value)
        side_lhs[span, 0:128] = top
        side_lhs[span, 128:256] = rest
        side_lhs[span, 256:384] = top
        return carry

    lax.fori_loop(0, SERIES, side_stage, 0)
    added = jnp.dot(side_lhs[...], side_weights[...], preferred_element_type=f32)
    fix[0] = added[:, :128]
    fix[1] = added[:, 128:]

    for side, there in ((0, has_north), (1, has_south)):
        @pl.when(there)
        def _(side=side):
            z_copy(side).wait_recv()

    def outer_stage(series, carry):
        centres, side_tiles = [], []
        for strip, index, edge, tiles, g in (
            (strip_n, 1, 1, (2, 3), SLOTS - 1), (strip_s, 3, 2, (0, 1), 0)
        ):
            for n, q in enumerate(tiles):
                value = strip[series, n * SLOTS : (n + 1) * SLOTS, :]
                centres.append(take(value, index))
                side = halo[edge, series, q, g : g + 1, :] * edge_mask[edge]
                side_tiles.append(take(value, index + 1) + side)
        stage(series, jnp.concatenate(centres, axis=0), side_tiles)
        return carry

    lax.fori_loop(0, SERIES, outer_stage, 0)
    filter_across((0, ROWS + 16))

    def add_fix(series, at, g, q):
        row = (series * 4 + q) * SLOTS + g
        span = pl.ds(at + 2 * SLOTS, SLOTS)
        m = fix_mask[...]
        across[series, span, :] = across[series, span, :] + fix[0, pl.ds(row, 1), :] * m
        swapped[series, span, :] = swapped[series, span, :] + fix[1, pl.ds(row, 1), :] * m

    def rim_fix(series, carry):
        for tile in (0, 1, TILES - 2, TILES - 1):
            add_fix(series, tile * SLOTS, tile // 4, tile % 4)
        return carry

    lax.fori_loop(0, SERIES, rim_fix, 0)

    first_half = lane < 64

    def filter_down(series, tile):
        base = tile * SLOTS
        m = live_mask[...]
        s = [across[series, pl.ds(base + SLOTS * n, SLOTS), :] for n in range(STEP + 4)]
        b = [swapped[series, pl.ds(base + SLOTS * n, SLOTS), :] for n in range(STEP + 4)]
        o = [jnp.where(first_half, b[n], b[n + 1]) for n in range(STEP + 3)]
        for n in range(STEP):
            total = (
                d[0] * s[n + 2] + d[1] * (o[n + 2] + o[n + 1]) + d[2] * (s[n + 3] + s[n + 1])
                + d[3] * (o[n + 3] + o[n]) + d[4] * (s[n + 4] + s[n])
            )
            done[series, pl.ds(base + SLOTS * n, SLOTS), :] = total * m

    def late_down(j, carry):
        def down_step(series, inner):
            filter_down(series, j * STEP)
            return inner

        return lax.fori_loop(0, SERIES, down_step, carry)

    def fixed_down(j, carry):
        first = bulk_row(j)

        def down_step(series, inner):
            for n in range(STEP):
                add_fix(series, first + n * SLOTS, j + (2 + n) // 4, (2 + n) % 4)
            filter_down(series, j * STEP)
            return inner

        return lax.fori_loop(0, SERIES, down_step, carry)

    lax.fori_loop(0, EARLY, fixed_down, 0)

    def bulk(j, carry):
        mix_chunk(j, carry)

        def sides_of(series, at, n):
            row = halo[0, series, (2 + n) % 4, pl.ds(j + (2 + n) // 4, 1), :]
            return own_side(series, at) + row * edge_mask[0]

        filter_across(stage_chunk(j, sides_of))

        @pl.when(j < CHUNKS - 1)
        def _():
            late_down(j, 0)

        return carry

    lax.fori_loop(EARLY, CHUNKS, bulk, 0)

    for side, there in ((0, has_right), (1, has_left)):
        @pl.when(there)
        def _(side=side):
            for item in range(3):
                y_copy(side, item).wait_send()

            def sent(j, carry):
                y_copy(side, j).wait_send()
                return carry

            lax.fori_loop(3, 3 + CHUNKS, sent, 0)

    for index, (dx, dz) in enumerate(PLACES):
        @pl.when(place_exists(dx, dz))
        def _(index=index):
            p_copy(index).wait_send()

    for side, there in ((0, has_south), (1, has_north)):
        @pl.when(there)
        def _(side=side):
            z_copy(side).wait_send()


def write_out(source, across, swapped, shared, target, rest, sems):
    first = (TILES - LAST) * SLOTS
    early = pltpu.make_async_copy(
        source.at[:, 0:first, :], target.at[:, 0:first, :], sems.at[SERIES]
    )
    early.start()
    m = shared[0:SLOTS, :]
    d = [shared[SLOTS + tap : SLOTS + tap + 1, :] for tap in range(5)]
    first_half = lax.broadcasted_iota(jnp.int32, (SLOTS, 128), 1) < 64
    copies = []
    for series in range(SERIES):
        spans = [slice(first + SLOTS * n, first + SLOTS * (n + 1)) for n in range(LAST + 4)]
        s = [across[series, span, :] for span in spans]
        b = [swapped[series, span, :] for span in spans]
        o = [jnp.where(first_half, b[n], b[n + 1]) for n in range(LAST + 3)]
        for n in range(LAST):
            total = (
                d[0] * s[n + 2] + d[1] * (o[n + 2] + o[n + 1]) + d[2] * (s[n + 3] + s[n + 1])
                + d[3] * (o[n + 3] + o[n]) + d[4] * (s[n + 4] + s[n])
            )
            rest[series, SLOTS * n : SLOTS * (n + 1), :] = total * m
        copy = pltpu.make_async_copy(
            rest.at[series], target.at[series, first:ROWS, :], sems.at[series]
        )
        copy.start()
        copies.append(copy)
    for copy in copies + [early]:
        copy.wait()


def shards(input_field, active_mask, neighbours, time_taps, space_taps, coregion_factor):
    shape = input_field.shape
    tiles = input_field.reshape(2, DAYS, SLOTS, TILES, 128).transpose(0, 1, 3, 2, 4)
    tiles = tiles.reshape(SERIES, ROWS, 128)
    f32 = jnp.float32
    vmem = pltpu.VMEM
    dma = pltpu.SemaphoreType.DMA
    parts = pl.pallas_call(
        kernel,
        out_shape=(
            vmem((SERIES, ROWS, 128), f32),
            vmem((SERIES, ROWS + 32, 128), f32),
            vmem((SERIES, ROWS + 32, 128), f32),
            vmem((2 * SLOTS, 128), f32),
        ),
        in_specs=[pl.BlockSpec(memory_space=pl.ANY)] * 6,
        out_specs=(pl.BlockSpec(memory_space=vmem),) * 4,
        scratch_shapes=[
            vmem((SERIES, ROWS, 128), f32),
            vmem((SERIES, ROWS, 128), f32),
            vmem((SERIES, ROWS, 128), f32),
            vmem((DAYS * SLOTS, 128), f32),
            vmem((DAYS * SLOTS, 128), f32),
            vmem((DAYS * SLOTS, 128), f32),
            vmem((DAYS * SLOTS, 128), f32),
            vmem((6, DAYS * SLOTS, 128), f32),
            vmem((SERIES, ROWS, 128), f32),
            vmem((SERIES, 16, 128), f32),
            vmem((SERIES, 16, 128), f32),
            vmem((3, SERIES, 4, SLOTS, 128), f32),
            vmem((3 * SERIES * STEP * SLOTS, 512), jnp.bfloat16),
            vmem((768, 256), jnp.bfloat16),
            vmem((SERIES * 4 * SLOTS, 384), jnp.bfloat16),
            vmem((384, 256), jnp.bfloat16),
            vmem((2, SERIES * 4 * SLOTS, 128), f32),
            vmem((5, SLOTS, 128), jnp.int32),
            vmem((5, SLOTS, 128), f32),
            vmem((3, SLOTS, 128), f32),
            vmem((SLOTS, 128), f32),
            vmem((SLOTS, 128), f32),
            vmem((SLOTS, 8), jnp.int32),
            pltpu.SMEM((SLOTS,), jnp.int32),
            pltpu.SMEM((DAYS + 1,), f32),
            pltpu.SMEM((2, 5), f32),
            pltpu.SMEM((2, 2), f32),
            dma,
            dma((5,)),
            dma((2, 3 + CHUNKS)),
            dma((2, 3 + CHUNKS)),
            dma((2,)),
            dma((2,)),
            dma((6,)),
            dma((6,)),
            pltpu.SemaphoreType.REGULAR,
            pltpu.SemaphoreType.REGULAR,
        ],
        compiler_params=pltpu.CompilerParams(collective_id=0, has_side_effects=True),
    )(tiles, neighbours, active_mask, time_taps, space_taps, coregion_factor)
    out = pl.pallas_call(
        write_out,
        out_shape=jax.ShapeDtypeStruct((SERIES, ROWS, 128), f32),
        in_specs=[pl.BlockSpec(memory_space=vmem)] * 4,
        out_specs=pl.BlockSpec(memory_space=pl.ANY),
        scratch_shapes=[vmem((SERIES, LAST * SLOTS, 128), f32), dma((SERIES + 1,))],
        name="write_out",
    )(*[pltpu.with_memory_space_constraint(part, vmem) for part in parts])
    out = out.reshape(2, DAYS, TILES, SLOTS, 128).transpose(0, 1, 3, 2, 4)
    return out.reshape(shape)


def solution(mesh):
    in_specs = (P(None, "day", "blk", None), P("blk"), P("blk", None), P(), P(), P())
    out_specs = P(None, "day", "blk", None)
    return jax.shard_map(shards, mesh=mesh, in_specs=in_specs, out_specs=out_specs, check_vma=False)
```
